32 devices in a mesh: slab: 2 (over x), inline: 8 (over z, y), xline: 2 (over core).
Axes of the slice: x: 2, y: 2, z: 4, core: 2. Of those that a mesh axis runs over, the one named last changes fastest.
Arguments:
- traces: bfloat16 [256, 48, 128], P(('slab', 'inline'), 'xline'), parts along dimension 0, may hold values from -15 to 15
- directions: int32 [10], replicated, may hold values from 0 to 31
- init_means: float32 [32, 20], replicated, may hold values from 0.3 to 2.5
- init_variances: float32 [32, 20], replicated, may hold values from 0.01 to 0.2
- init_weights: float32 [32], replicated, may hold values from 0.01 to 1
Outputs:
- posterior: bfloat16 [256, 32, 48, 128], P(('slab', 'inline'), None, 'xline'), parts along dimension 0
- final_means: float32 [64, 20], P('slab'), parts along dimension 0
- final_variances: float32 [64, 20], P('slab'), parts along dimension 0
- final_weights: float32 [64], P('slab'), parts along dimension 0
The draws below stay inside these ranges and needn't reach their ends.
There are 2 independent parts, one for each index of `slab`. The reference program is written for one: setup_inputs(seed, part) draws one part's arguments, and reference() takes and returns one part's arrays. A program takes and returns all parts, laid end to end along the dimension named above; an argument that names none is the same for every part. Nothing has to cross between parts.
All inputs are finite; a program needn't handle non-finite values.
Results may differ from the reference program's by a relative error of at most 0.001.
The reference program's roundings to bfloat16 on the way count: a program that leaves them out, or rounds other values in their place, can miss the bound.
Values may be sent and summed in bfloat16 or wider, within the bound.
A program may use at most 64 MiB of HBM per device.

```python
import math
import jax
import jax.numpy as jnp
import numpy as np
from jax import lax

NT = 128
ORIENTS = 10
FEATS = 20
K = 32
TAPS = 31
HALF = 15
AZIMUTHS = 8
DIPS = 4
ITERS = 2
NI = 128
NX = 48
CELLS = 786432


def draw_traces(key, part):
    position = jnp.arange(NI).astype(jnp.float32) / max(NI - 1, 1)
    drawn_values = jnp.clip(jax.random.normal(key, (NI, NX, NT), jnp.float32), -5.0, 5.0)
    amplitude = 3.0 ** position
    return jnp.clip(drawn_values * amplitude[:, None, None], -15.0, 15.0).astype(jnp.bfloat16)


def set_ends(values, key, smallest, high):
    shape = values.shape
    place = [jax.random.randint(jax.random.fold_in(key, axis), (), 0, shape[axis]) for axis in range(len(shape))]
    values = values.at[tuple(place)].set(smallest)
    longest = shape.index(max(shape))
    place[longest] = (place[longest] + 1) % shape[longest]
    return values.at[tuple(place)].set(high)


def setup_inputs(seed: int = 0, part: int = 0) -> dict:
    seeds = jax.random.split(jax.random.key(seed), 6)
    part_keys = jax.random.split(jax.random.fold_in(seeds[5], part), 6)
    return {
        "traces": draw_traces(jax.random.fold_in(jax.random.fold_in(seeds[5], part), 71), part),
        "directions": set_ends(jax.random.randint(seeds[1], (ORIENTS,), 0, AZIMUTHS * DIPS), jax.random.fold_in(seeds[1], 1), 0, (AZIMUTHS * DIPS) - 1).astype(jnp.int32),
        "init_means": jnp.clip(jax.random.uniform(seeds[2], (K, FEATS), jnp.float32, 0.3, 2.5), 0.3, 2.5),
        "init_variances": jnp.clip(jnp.exp(jax.random.uniform(seeds[3], (K, FEATS), jnp.float32, math.log(0.01), math.log(0.2))), 0.01, 0.2),
        "init_weights": jnp.clip(jnp.exp(jax.random.uniform(seeds[4], (K,), jnp.float32, math.log(0.01), math.log(1.0))), 0.01, 1.0),
    }


eps_mag = 0.01
wavenumber = math.pi / 4.0
highest = lax.Precision.HIGHEST
cross_real = np.array([[[1.0, 0.0], [1.0, 0.0]], [[0.0, 1.0], [0.0, -1.0]]], np.float32)
cross_imag = np.array([[[0.0, 1.0], [0.0, 1.0]], [[-1.0, 0.0], [1.0, 0.0]]], np.float32)

def tap_table(directions):
    azimuth = (directions % AZIMUTHS).astype(jnp.float32) * (math.pi / AZIMUTHS)
    dip_angle = (directions // AZIMUTHS + 1).astype(jnp.float32) * (math.pi / (2 * DIPS + 2))
    wave_vector = wavenumber * jnp.stack([jnp.sin(dip_angle) * jnp.cos(azimuth), jnp.sin(dip_angle) * jnp.sin(azimuth), jnp.cos(dip_angle)], axis=1)
    offsets = jnp.arange(TAPS).astype(jnp.float32) - HALF
    width_scale = HALF / 3.0
    envelope = jnp.exp(-offsets * offsets / (2.0 * width_scale * width_scale))
    envelope = envelope / jnp.sqrt(jnp.sum(envelope * envelope))
    phases = wave_vector[:, :, None] * offsets[None, None, :]
    return jnp.stack([envelope * jnp.cos(phases), envelope * jnp.sin(phases)], axis=2).astype(jnp.bfloat16)

def band_onehot(rows_in, rows_out, offset_base):
    difference = jnp.arange(rows_in).astype(jnp.int32)[:, None] - jnp.arange(rows_out).astype(jnp.int32)[None, :] + offset_base
    return (difference[:, :, None] == jnp.arange(TAPS).astype(jnp.int32)[None, None, :]).astype(jnp.float32)

def log_scores(feature_rows, centers, spreads, log_weights):
    inverse = 1.0 / spreads
    offset_term = log_weights - 0.5 * lax.optimization_barrier(jnp.sum(jnp.log(2.0 * math.pi * spreads), axis=1))
    distance = lax.optimization_barrier(jnp.sum((feature_rows[None, :, :] - centers[:, :, None]) ** 2 * inverse[:, :, None], axis=1))
    return offset_term[:, None] - 0.5 * distance

def posterior_weights(feature_rows, centers, spreads, log_weights):
    scores = log_scores(feature_rows, centers, spreads, log_weights)
    largest = lax.optimization_barrier(jnp.max(scores, axis=0, keepdims=True))
    exponent = jnp.exp(scores - largest)
    return exponent / lax.optimization_barrier(jnp.sum(exponent, axis=0, keepdims=True))

def first_pass(feature_rows, centers, spreads, log_weights):
    posterior = posterior_weights(feature_rows, centers, spreads, log_weights)
    return (posterior.astype(jnp.bfloat16), lax.optimization_barrier(jnp.sum(posterior, axis=1)), jnp.einsum('km,fm->kf', posterior, feature_rows, precision=highest))

def centred_pass(feature_rows, centers, spreads, log_weights, new_centers):
    posterior = posterior_weights(feature_rows, centers, spreads, log_weights)
    return lax.optimization_barrier(jnp.sum(posterior[:, None, :] * (feature_rows[None, :, :] - new_centers[:, :, None]) ** 2, axis=2))

def reference(traces, directions, init_means, init_variances, init_weights):
    tap_values = tap_table(directions)
    wide_taps = tap_values.astype(jnp.float32)
    time_mats = jnp.einsum('stn,orn->osrt', band_onehot(NT, NT, HALF), wide_taps[:, 2], precision=highest).astype(jnp.bfloat16)
    xline_taps = jnp.einsum('pqr,on->opqrn', cross_real, wide_taps[:, 1, 0]) + jnp.einsum('pqr,on->opqrn', cross_imag, wide_taps[:, 1, 1])
    xline_mats = jnp.einsum('xyn,opqrn->oxpqry', band_onehot(NX, NX, HALF), xline_taps, precision=highest).astype(jnp.bfloat16)
    inline_taps = tap_values[:, 0]
    flat_traces = traces.reshape(NI * NX, NT)

    def orient_features(pieces):
        time_one, xline_one, inline_one = pieces
        band = jnp.dot(flat_traces, time_one.reshape(NT, 2 * NT), preferred_element_type=jnp.float32)
        band = band.astype(jnp.bfloat16).reshape(NI, NX, 2, NT)
        across = jnp.einsum('ixpt,xpqry->iqryt', band.astype(jnp.float32), xline_one.astype(jnp.float32), precision=highest).astype(jnp.bfloat16)
        padded = jnp.pad(across.astype(jnp.float32), ((HALF, HALF), (0, 0), (0, 0), (0, 0), (0, 0)))
        real_part = jnp.zeros((NI, 2, NX, NT), jnp.float32)
        imag_part = jnp.zeros((NI, 2, NX, NT), jnp.float32)
        for shift_index in range(TAPS):
            window = padded[shift_index:shift_index + NI]
            tap_real = inline_one[0, shift_index].astype(jnp.float32)
            tap_imag = inline_one[1, shift_index].astype(jnp.float32)
            real_part = real_part + window[:, :, 0] * tap_real - window[:, :, 1] * tap_imag
            imag_part = imag_part + window[:, :, 0] * tap_imag + window[:, :, 1] * tap_real
        return jnp.sqrt(real_part * real_part + imag_part * imag_part + eps_mag)
    stacked = lax.map(orient_features, (time_mats, xline_mats, inline_taps))
    features = jnp.transpose(stacked, (1, 0, 2, 3, 4)).reshape(NI, FEATS, NX * NT)
    centers = init_means
    spreads = init_variances
    weights = init_weights
    log_weights = jnp.log(init_weights)
    posterior = None
    for iteration in range(ITERS):
        posterior, masses, firsts = lax.map(lambda feature_rows: first_pass(feature_rows, centers, spreads, log_weights), features)
        total_mass = lax.optimization_barrier(jnp.sum(masses, axis=0))
        total_first = lax.optimization_barrier(jnp.sum(firsts, axis=0))
        new_centers = (total_first + centers) / (total_mass + 1.0)[:, None]
        spread_rows = lax.map(lambda feature_rows: centred_pass(feature_rows, centers, spreads, log_weights, new_centers), features)
        new_spreads = (lax.optimization_barrier(jnp.sum(spread_rows, axis=0)) + spreads) / (total_mass + 1.0)[:, None]
        weights = (total_mass + 1.0) / (CELLS + K)
        log_weights = jnp.log(weights)
        centers = new_centers
        spreads = new_spreads
    return (posterior.reshape(NI, K, NX, NT), centers, spreads, weights)
```

```python
import functools
import math

import jax
import jax.numpy as jnp
from jax import lax
from jax.experimental import pallas as pl
from jax.experimental.pallas import tpu as pltpu
from jax.sharding import PartitionSpec as P

TAPS = 31
HALF = 15
AZIMUTHS = 8
DIPS = 4
ITERS = 2
LANES = 128

eps_mag = 0.01
wavenumber = math.pi / 4.0
MESH = pl.DeviceIdType.MESH
f32 = jnp.float32
bf16 = jnp.bfloat16
VMEM = pltpu.MemorySpace.VMEM
SMEM = pltpu.MemorySpace.SMEM


def round_up(value, step):
    return -(-value // step) * step


def tap_table(directions):
    azimuth = (directions % AZIMUTHS).astype(f32) * (math.pi / AZIMUTHS)
    dip_angle = (directions // AZIMUTHS + 1).astype(f32) * (math.pi / (2 * DIPS + 2))
    wave_vector = wavenumber * jnp.stack(
        [
            jnp.sin(dip_angle) * jnp.cos(azimuth),
            jnp.sin(dip_angle) * jnp.sin(azimuth),
            jnp.cos(dip_angle),
        ],
        axis=1,
    )
    offsets = jnp.arange(TAPS).astype(f32) - HALF
    width_scale = HALF / 3.0
    envelope = jnp.exp(-offsets * offsets / (2.0 * width_scale * width_scale))
    envelope = envelope / jnp.sqrt(jnp.sum(envelope * envelope))
    phases = wave_vector[:, :, None] * offsets[None, None, :]
    return jnp.stack([envelope * jnp.cos(phases), envelope * jnp.sin(phases)], axis=2)


def halo_kernel(inlines, xlines, own_ref, out_ref, send_sem, recv_sem):
    row = lax.axis_index("inline")
    col = lax.axis_index("xline")
    steps = [
        (side, shift)
        for side in (-1, 0, 1)
        for shift in range(xlines)
        if not (side == 0 and shift == 0)
    ]

    def there(side):
        if side == 0:
            return row >= 0
        return row > 0 if side < 0 else row < inlines - 1

    def peer(side, shift):
        return {"inline": row + side, "xline": lax.rem(col + shift, xlines)}

    barrier = pltpu.get_barrier_semaphore()
    for side, shift in steps:
        @pl.when(there(side))
        def _(side=side, shift=shift):
            pl.semaphore_signal(barrier, inc=1, device_id=peer(side, shift), device_id_type=MESH)
    sides = 1 + (row > 0).astype(jnp.int32) + (row < inlines - 1).astype(jnp.int32)
    pl.semaphore_wait(barrier, sides * xlines - 1)

    def copy(side, shift):
        return pltpu.make_async_remote_copy(
            src_ref=own_ref,
            dst_ref=out_ref.at[1 - side, col],
            send_sem=send_sem.at[1 - side, shift],
            recv_sem=recv_sem.at[1 - side, shift],
            device_id=peer(side, shift),
            device_id_type=MESH,
        )

    for side, shift in steps:
        @pl.when(there(side))
        def _(side=side, shift=shift):
            copy(side, shift).start()
    out_ref[1, col] = own_ref[...]
    for side in (-1, 1):
        @pl.when(jnp.logical_not(there(side)))
        def _(side=side):
            out_ref[1 + side] = jnp.zeros(out_ref.shape[1:], out_ref.dtype)
    for side, shift in steps:
        @pl.when(there(side))
        def _(side=side, shift=shift):
            copy(side, shift).wait_send()
        @pl.when(there(-side))
        def _(side=side, shift=shift):
            copy(side, shift).wait_recv()


def gather_halo(traces):
    inlines, xlines = lax.axis_size("inline"), lax.axis_size("xline")
    return pl.pallas_call(
        functools.partial(halo_kernel, inlines, xlines),
        out_shape=jax.ShapeDtypeStruct((3, xlines) + traces.shape, traces.dtype),
        in_specs=[pl.BlockSpec(memory_space=VMEM)],
        out_specs=pl.BlockSpec(memory_space=VMEM),
        scratch_shapes=[
            pltpu.SemaphoreType.DMA((3, xlines)),
            pltpu.SemaphoreType.DMA((3, xlines)),
        ],
        compiler_params=pltpu.CompilerParams(collective_id=0, has_side_effects=True),
        name="halo",
    )(traces)


def filter_kernel(sizes, taps_ref, place_ref, halo_ref, out_ref, flat, cross):
    rows, cols, width, pad, orients = sizes
    deep = 3 * rows
    group = 4 if deep % 4 == 0 else 1
    orient = pl.program_id(0)

    @pl.when(orient == 0)
    def _():
        for block in range(3):
            for i in range(rows):
                for part in range(width // cols):
                    start = ((block * rows + i) * width) + part * cols
                    flat[start : start + cols, :] = halo_ref[block, part, i].astype(f32)
        for y in range(cols):
            for extra in range(pad - 2 * orients):
                out_ref[y, pl.ds(2 * orients + extra, rows, stride=pad), :] = jnp.full(
                    (rows, LANES), 1.0 if extra == 0 else 0.0, f32
                )

    def tap(axis, part, n):
        return taps_ref[((orient * 3 + axis) * 2 + part) * TAPS + n]

    def toeplitz(axis, difference):
        real = jnp.zeros(difference.shape, f32)
        imag = jnp.zeros(difference.shape, f32)
        for n in range(TAPS):
            hit = difference == n
            real = jnp.where(hit, tap(axis, 0, n), real)
            imag = jnp.where(hit, tap(axis, 1, n), imag)
        return real, imag

    def iotas(shape):
        return (
            lax.broadcasted_iota(jnp.int32, shape, 0),
            lax.broadcasted_iota(jnp.int32, shape, 1),
        )

    source, target = iotas((LANES, LANES))
    real, imag = toeplitz(2, source - target + HALF)
    time_mat = jnp.concatenate([real, imag], axis=1).astype(bf16)

    lanes = 2 * LANES
    y, x = iotas((cols, lanes))
    difference = jnp.where(x < width, x - y - place_ref[0] + HALF, -1)
    real, imag = toeplitz(1, difference)
    base = jnp.concatenate([real, imag], axis=0)
    x_mat = jnp.concatenate(
        [base if g == 0 else pltpu.roll(base, g * width, 1) for g in range(group)], axis=0
    ).astype(bf16)[:, : group * width]

    j, i = iotas((rows, lanes))
    real_first, imag_first = toeplitz(0, jnp.where(i < deep, i - j - rows + HALF, -1))
    real_next, imag_next = pltpu.roll(real_first, deep, 1), pltpu.roll(imag_first, deep, 1)
    base = jnp.concatenate([real_first - imag_next, imag_first + real_next], axis=0)
    i_mat = jnp.concatenate([base, pltpu.roll(base, 2 * deep, 1)], axis=0).astype(bf16)
    i_mat = i_mat[:, : 4 * deep]

    for step in range(deep // group):
        span = group * width
        band = jnp.dot(
            flat[step * span : (step + 1) * span, :].astype(bf16),
            time_mat,
            preferred_element_type=f32,
        ).astype(bf16)
        mixed = jnp.dot(x_mat, band, preferred_element_type=f32)
        for g in range(group):
            i_row = step * group + g
            first = g * 2 * cols
            with_cos = mixed[first : first + cols]
            with_sin = mixed[first + cols : first + 2 * cols]
            cu, cv = with_cos[:, :LANES], with_cos[:, LANES:]
            su, sv = with_sin[:, :LANES], with_sin[:, LANES:]
            for slot, value in enumerate((cu - sv, su + cv, cu + sv, su - cv)):
                cross[pl.ds(slot * cols * deep + i_row, cols, stride=deep), :] = value

    half = cols // 2
    for q in range(2):
        for y0 in range(0, half, 2):
            columns = []
            for dy in range(2):
                pieces = []
                for g in range(2):
                    for r in range(2):
                        start = ((q * 2 + r) * cols + y0 + dy + g * half) * deep
                        pieces.append(cross[start : start + deep, :])
                columns.append(jnp.concatenate(pieces, axis=0).astype(bf16))
            total = jnp.dot(i_mat, jnp.concatenate(columns, axis=1), preferred_element_type=f32)
            for g in range(2):
                re = total[g * 2 * rows : g * 2 * rows + rows]
                im = total[g * 2 * rows + rows : (g + 1) * 2 * rows]
                size = jnp.sqrt(re * re + im * im + eps_mag)
                for dy in range(2):
                    out_ref[
                        y0 + dy + g * half, pl.ds(2 * orient + q, rows, stride=pad), :
                    ] = size[:, dy * LANES : (dy + 1) * LANES]


def filter_features(halo, taps, place, pad):
    _, xlines, rows, cols, samples = halo.shape
    orients = taps.shape[0]
    width = xlines * cols
    sizes = (rows, cols, width, pad, orients)
    return pl.pallas_call(
        functools.partial(filter_kernel, sizes),
        out_shape=jax.ShapeDtypeStruct((cols, rows * pad, samples), f32),
        grid=(orients,),
        in_specs=[
            pl.BlockSpec(memory_space=SMEM),
            pl.BlockSpec(memory_space=SMEM),
            pl.BlockSpec(halo.shape, lambda o: (0,) * 5),
        ],
        out_specs=pl.BlockSpec((cols, rows * pad, samples), lambda o: (0, 0, 0)),
        scratch_shapes=[
            pltpu.VMEM((3 * rows * width, samples), f32),
            pltpu.VMEM((4 * cols * 3 * rows, samples), f32),
        ],
        compiler_params=pltpu.CompilerParams(vmem_limit_bytes=50 << 20),
        name="filters",
    )(taps.reshape(-1), place, halo)


def split3(value):
    high = value.astype(bf16)
    rest = value - high.astype(f32)
    mid = rest.astype(bf16)
    low = (rest - mid.astype(f32)).astype(bf16)
    return high, mid, low


def moment_kernel(sizes, with_posterior, feat_ref, shift_ref, mean_ref, var_ref, weight_ref, *rest):
    cols, pad, count, chunk = sizes
    if with_posterior:
        moment_ref, post_ref, table, total, wide = rest
    else:
        moment_ref, table, total = rest
    step = pl.program_id(0)
    comps = mean_ref.shape[0]

    @pl.when(step == 0)
    def _():
        lane = lax.broadcasted_iota(jnp.int32, (comps, 2 * LANES), 1)
        means = jnp.concatenate([mean_ref[...], jnp.zeros((comps, LANES), f32)], axis=1)
        spreads = jnp.concatenate([var_ref[...], jnp.ones((comps, LANES), f32)], axis=1)
        used = lane < count
        inverse = jnp.where(used, 1.0 / spreads, 0.0)
        scaled = means * inverse
        terms = jnp.where(used, jnp.log(2.0 * math.pi * spreads) + means * scaled, 0.0)
        constant = jnp.log(weight_ref[:, :1]) - 0.5 * jnp.sum(terms, axis=1, keepdims=True)
        row = jnp.where(used, scaled, 0.0) + jnp.where(lane == count, constant, 0.0)
        row = row + pltpu.roll(-0.5 * inverse, pad, 1)
        parts = split3(row)
        for index, part in enumerate(parts):
            part = part.astype(f32)
            tiled = part + pltpu.roll(part, 2 * pad, 1) + pltpu.roll(part, 4 * pad, 1)
            table[index * comps : (index + 1) * comps, :] = tiled.astype(bf16)
        total[...] = jnp.zeros_like(total)

    weights = table[:, : 6 * pad]
    for first in range(0, cols, chunk):
        values = jnp.concatenate(
            [feat_ref[first + y] - shift_ref[...] for y in range(chunk)], axis=1
        )
        both = jnp.concatenate([values, values * values], axis=0)
        operand = jnp.concatenate(split3(both), axis=0)
        wide_score = jnp.dot(weights, operand, preferred_element_type=f32)
        score = wide_score[:comps] + (
            wide_score[comps : 2 * comps] + wide_score[2 * comps : 3 * comps]
        )
        exponent = jnp.exp(score - jnp.max(score, axis=0, keepdims=True))
        share = exponent * (1.0 / jnp.sum(exponent, axis=0, keepdims=True))
        high = share.astype(bf16)
        low = (share - high.astype(f32)).astype(bf16)
        total[...] += lax.dot_general(
            jnp.concatenate([high, low], axis=0),
            operand,
            (((1,), (1,)), ((), ())),
            preferred_element_type=f32,
        )
        if with_posterior:
            for y in range(chunk):
                wide[pl.ds(first + y, comps, stride=cols), :] = share[
                    :, y * LANES : (y + 1) * LANES
                ]
    if with_posterior:
        for k in range(comps):
            post_ref[0, k] = wide[k * cols : (k + 1) * cols, :].astype(bf16)

    @pl.when(step == pl.num_programs(0) - 1)
    def _():
        both = total[:comps] + total[comps:]
        both = jnp.concatenate([both, jnp.zeros((comps, 2 * LANES - 6 * pad), f32)], axis=1)
        folded = (
            both
            + pltpu.roll(both, 2 * LANES - 2 * pad, 1)
            + pltpu.roll(both, 2 * LANES - 4 * pad, 1)
        )
        moment_ref[...] = folded[:, :LANES]


def moments(features, shift, params, count, rows, with_posterior):
    means, spreads, weights = params
    comps = means.shape[0]
    cols, flat, samples = features.shape
    pad = flat // rows
    chunk = 4 if cols % 4 == 0 else 1
    whole = lambda array: pl.BlockSpec(array.shape, lambda j: (0, 0))
    out_shape = [jax.ShapeDtypeStruct((comps, LANES), f32)]
    out_specs = [pl.BlockSpec((comps, LANES), lambda j: (0, 0))]
    scratch = [pltpu.VMEM((3 * comps, 2 * LANES), bf16), pltpu.VMEM((2 * comps, 6 * pad), f32)]
    if with_posterior:
        out_shape.append(jax.ShapeDtypeStruct((rows, comps, cols, samples), bf16))
        out_specs.append(pl.BlockSpec((1, comps, cols, samples), lambda j: (j, 0, 0, 0)))
        scratch.append(pltpu.VMEM((comps * cols, samples), f32))
    return pl.pallas_call(
        functools.partial(moment_kernel, (cols, pad, count, chunk), with_posterior),
        out_shape=out_shape,
        grid=(rows,),
        in_specs=[
            pl.BlockSpec((cols, pad, samples), lambda j: (0, j, 0)),
            whole(shift),
            whole(means),
            whole(spreads),
            whole(weights),
        ],
        out_specs=out_specs,
        scratch_shapes=scratch,
        compiler_params=pltpu.CompilerParams(vmem_limit_bytes=50 << 20),
        name="last_pass" if with_posterior else "first_pass",
    )(features, shift, means, spreads, weights)


def update_kernel(
    sizes, moment_ref, mean_ref, var_ref, mean_out, var_out, weight_out, slots, send_sem, recv_sem
):
    inlines, xlines, pad, count, cells = sizes
    members = inlines * xlines
    comps = mean_ref.shape[0]
    me = lax.axis_index("inline") * xlines + lax.axis_index("xline")

    def peer(shift):
        other = lax.rem(me + shift, members)
        return {"inline": other // xlines, "xline": lax.rem(other, xlines)}

    barrier = pltpu.get_barrier_semaphore()
    for shift in range(1, members):
        pl.semaphore_signal(barrier, inc=1, device_id=peer(shift), device_id_type=MESH)
    pl.semaphore_wait(barrier, members - 1)

    def copy(shift):
        return pltpu.make_async_remote_copy(
            src_ref=moment_ref,
            dst_ref=slots.at[me],
            send_sem=send_sem.at[shift],
            recv_sem=recv_sem.at[shift],
            device_id=peer(shift),
            device_id_type=MESH,
        )

    for shift in range(1, members):
        copy(shift).start()
    slots[me] = moment_ref[...]
    for shift in range(1, members):
        copy(shift).wait()
    total = slots[0]
    for member in range(1, members):
        total = total + slots[member]
    mass = total[:, count : count + 1]
    means, spreads = mean_ref[...], var_ref[...]
    used = lax.broadcasted_iota(jnp.int32, (comps, LANES), 1) < count
    first = jnp.where(used, total, 0.0)
    second = jnp.where(used, pltpu.roll(total, LANES - pad, 1), 0.0)
    below = mass + 1.0
    new_means = (first + means) / below
    centred = second - 2.0 * new_means * first + new_means * new_means * mass
    mean_out[...] = new_means
    var_out[...] = jnp.where(used, (centred + spreads) / below, 1.0)
    weight_out[...] = jnp.broadcast_to(below / (cells + comps), (comps, LANES))


def update(moment, params, pad, count, cells, collective_id):
    means, spreads, _ = params
    inlines, xlines = lax.axis_size("inline"), lax.axis_size("xline")
    members = inlines * xlines
    comps = means.shape[0]
    return pl.pallas_call(
        functools.partial(update_kernel, (inlines, xlines, pad, count, cells)),
        out_shape=[jax.ShapeDtypeStruct((comps, LANES), f32)] * 3,
        in_specs=[pl.BlockSpec(memory_space=VMEM)] * 3,
        out_specs=[pl.BlockSpec(memory_space=VMEM)] * 3,
        scratch_shapes=[
            pltpu.VMEM((members, comps, LANES), f32),
            pltpu.SemaphoreType.DMA((members,)),
            pltpu.SemaphoreType.DMA((members,)),
        ],
        compiler_params=pltpu.CompilerParams(
            collective_id=collective_id, has_side_effects=True
        ),
        name="update",
    )(moment, means, spreads)


def per_device(traces, directions, init_means, init_variances, init_weights):
    rows, cols, samples = traces.shape
    assert samples == LANES and rows >= HALF
    orients = directions.shape[0]
    count = 2 * orients
    pad = round_up(count + 1, 8)
    comps = init_weights.shape[0]
    cells = lax.axis_size("inline") * rows * lax.axis_size("xline") * cols * samples
    taps = tap_table(directions)
    place = (lax.axis_index("xline") * cols).astype(jnp.int32).reshape(1)
    shift_row = jnp.mean(init_means, axis=0)
    shift = jnp.broadcast_to(jnp.pad(shift_row, (0, pad - count))[:, None], (pad, LANES))
    halo = gather_halo(traces)
    features = filter_features(halo, taps, place, pad)
    means = jnp.pad(init_means - shift_row, ((0, 0), (0, LANES - count)))
    spreads = jnp.pad(init_variances, ((0, 0), (0, LANES - count)), constant_values=1.0)
    params = (means, spreads, jnp.broadcast_to(init_weights[:, None], (comps, LANES)))
    posterior = None
    for iteration in range(ITERS):
        last = iteration == ITERS - 1
        results = moments(features, shift, params, count, rows, last)
        if last:
            posterior = results[1]
        params = update(results[0], params, pad, count, cells, 1 + iteration)
    means, spreads, weights = params
    return posterior, means[:, :count] + shift_row, spreads[:, :count], weights[:, 0]


def solution(mesh):
    in_specs = (P(("slab", "inline"), "xline", None), P(), P(), P(), P())
    out_specs = (
        P(("slab", "inline"), None, "xline", None),
        P("slab", None),
        P("slab", None),
        P("slab"),
    )
    return jax.shard_map(
        per_device, mesh=mesh, in_specs=in_specs, out_specs=out_specs, check_vma=False
    )
```

```python
import functools
import math

import jax
import jax.numpy as jnp
from jax import lax
from jax.experimental import pallas as pl
from jax.experimental.pallas import tpu as pltpu
from jax.sharding import PartitionSpec as P

TAPS = 31
HALF = 15
AZIMUTHS = 8
DIPS = 4
ITERS = 2
LANES = 128

eps_mag = 0.01
wavenumber = math.pi / 4.0
MESH = pl.DeviceIdType.MESH
f32 = jnp.float32
bf16 = jnp.bfloat16
VMEM = pltpu.MemorySpace.VMEM
SMEM = pltpu.MemorySpace.SMEM


def round_up(value, step):
    return -(-value // step) * step


def tap_table(directions):
    azimuth = (directions % AZIMUTHS).astype(f32) * (math.pi / AZIMUTHS)
    dip_angle = (directions // AZIMUTHS + 1).astype(f32) * (math.pi / (2 * DIPS + 2))
    wave_vector = wavenumber * jnp.stack(
        [
            jnp.sin(dip_angle) * jnp.cos(azimuth),
            jnp.sin(dip_angle) * jnp.sin(azimuth),
            jnp.cos(dip_angle),
        ],
        axis=1,
    )
    offsets = jnp.arange(TAPS).astype(f32) - HALF
    width_scale = HALF / 3.0
    envelope = jnp.exp(-offsets * offsets / (2.0 * width_scale * width_scale))
    envelope = envelope / jnp.sqrt(jnp.sum(envelope * envelope))
    phases = wave_vector[:, :, None] * offsets[None, None, :]
    return jnp.stack([envelope * jnp.cos(phases), envelope * jnp.sin(phases)], axis=2)


def halo_kernel(inlines, xlines, own_ref, out_ref, send_sem, recv_sem):
    row = lax.axis_index("inline")
    col = lax.axis_index("xline")
    steps = [
        (side, shift)
        for side in (-1, 0, 1)
        for shift in range(xlines)
        if not (side == 0 and shift == 0)
    ]

    def there(side):
        if side == 0:
            return row >= 0
        return row > 0 if side < 0 else row < inlines - 1

    def peer(side, shift):
        return {"inline": row + side, "xline": lax.rem(col + shift, xlines)}

    barrier = pltpu.get_barrier_semaphore()
    for side, shift in steps:
        @pl.when(there(side))
        def _(side=side, shift=shift):
            pl.semaphore_signal(barrier, inc=1, device_id=peer(side, shift), device_id_type=MESH)
    sides = 1 + (row > 0).astype(jnp.int32) + (row < inlines - 1).astype(jnp.int32)
    pl.semaphore_wait(barrier, sides * xlines - 1)

    def copy(side, shift):
        return pltpu.make_async_remote_copy(
            src_ref=own_ref,
            dst_ref=out_ref.at[1 - side, col],
            send_sem=send_sem.at[1 - side, shift],
            recv_sem=recv_sem.at[1 - side, shift],
            device_id=peer(side, shift),
            device_id_type=MESH,
        )

    for side, shift in steps:
        @pl.when(there(side))
        def _(side=side, shift=shift):
            copy(side, shift).start()
    out_ref[1, col] = own_ref[...]
    for side in (-1, 1):
        @pl.when(jnp.logical_not(there(side)))
        def _(side=side):
            out_ref[1 + side] = jnp.zeros(out_ref.shape[1:], out_ref.dtype)
    for side, shift in steps:
        @pl.when(there(side))
        def _(side=side, shift=shift):
            copy(side, shift).wait_send()
        @pl.when(there(-side))
        def _(side=side, shift=shift):
            copy(side, shift).wait_recv()


def gather_halo(traces):
    inlines, xlines = lax.axis_size("inline"), lax.axis_size("xline")
    return pl.pallas_call(
        functools.partial(halo_kernel, inlines, xlines),
        out_shape=jax.ShapeDtypeStruct((3, xlines) + traces.shape, traces.dtype),
        in_specs=[pl.BlockSpec(memory_space=VMEM)],
        out_specs=pl.BlockSpec(memory_space=VMEM),
        scratch_shapes=[
            pltpu.SemaphoreType.DMA((3, xlines)),
            pltpu.SemaphoreType.DMA((3, xlines)),
        ],
        compiler_params=pltpu.CompilerParams(collective_id=0, has_side_effects=True),
        name="halo",
    )(traces)


def filter_kernel(sizes, taps_ref, place_ref, halo_ref, out_ref, flat, x_mat, cross):
    rows, cols, width, pad, orients = sizes
    deep = 3 * rows
    group = 8
    orient = pl.program_id(0)

    @pl.when(orient == 0)
    def _():
        for block in range(3):
            for i in range(rows):
                for part in range(width // cols):
                    start = ((block * rows + i) * width) + part * cols
                    flat[start : start + cols, :] = halo_ref[block, part, i]
        for y in range(cols):
            for extra in range(pad - 2 * orients):
                out_ref[y, pl.ds(2 * orients + extra, rows, stride=pad), :] = jnp.full(
                    (rows, LANES), 1.0 if extra == 0 else 0.0, f32
                )

    def tap(axis, part, n):
        return taps_ref[((orient * 3 + axis) * 2 + part) * TAPS + n]

    def toeplitz(axis, difference):
        real = jnp.zeros(difference.shape, f32)
        imag = jnp.zeros(difference.shape, f32)
        for n in range(TAPS):
            hit = difference == n
            real = jnp.where(hit, tap(axis, 0, n), real)
            imag = jnp.where(hit, tap(axis, 1, n), imag)
        return real, imag

    def iotas(shape):
        return (
            lax.broadcasted_iota(jnp.int32, shape, 0),
            lax.broadcasted_iota(jnp.int32, shape, 1),
        )

    def roll(value, amount):
        return value if amount == 0 else pltpu.roll(value, amount, 1)

    sub, lane = iotas((8, LANES))
    bases = toeplitz(2, jnp.bitwise_and(sub - lane + HALF, LANES - 1))
    pieces = []
    for s in range(0, LANES, 8):
        near = jnp.abs(sub + s - lane) <= HALF
        pieces.append(
            jnp.concatenate([jnp.where(near, roll(base, s), 0.0) for base in bases], axis=1)
        )
    time_mat = jnp.concatenate(pieces, axis=0).astype(bf16)

    lanes = round_up(group * width + LANES, LANES)
    sub, lane = iotas((group, lanes))
    difference = lane - sub * width - place_ref[0] + HALF
    bases = toeplitz(1, jnp.where(difference >= lanes - 64, difference - lanes, difference))
    mine = jnp.logical_and(lane >= sub * width, lane < (sub + 1) * width)
    for part in range(2):
        for y in range(0, cols, 2):
            pair = jnp.concatenate(
                [jnp.where(mine, roll(bases[part], y + dy), 0.0) for dy in range(2)], axis=0
            )
            start = (part * cols + y) * group
            x_mat[start : start + 2 * group, :] = pair[:, : group * width].astype(bf16)

    sub, lane = iotas((8, LANES))
    bases = toeplitz(0, jnp.bitwise_and(lane - sub - rows + HALF, LANES - 1))
    real_first, imag_first = [
        jnp.concatenate(
            [jnp.where(lane < deep, roll(base, j), 0.0) for j in range(0, rows, 8)], axis=0
        )
        for base in bases
    ]
    blank = jnp.zeros((rows, LANES), f32)
    real_first, imag_first = [
        jnp.concatenate([part, blank], axis=1) for part in (real_first, imag_first)
    ]
    real_next, imag_next = pltpu.roll(real_first, deep, 1), pltpu.roll(imag_first, deep, 1)
    base = jnp.concatenate([real_first - imag_next, imag_first + real_next], axis=0)
    i_mat = jnp.concatenate([base, pltpu.roll(base, 2 * deep, 1)], axis=0).astype(bf16)
    i_mat = i_mat[:, : 4 * deep]

    for step in range(deep // group):
        span = group * width
        band = jnp.dot(
            flat[step * span : (step + 1) * span, :],
            time_mat,
            preferred_element_type=f32,
        ).astype(bf16)
        mixed = jnp.dot(x_mat[...], band, preferred_element_type=f32)
        for y in range(cols):
            with_cos = mixed[y * group : (y + 1) * group]
            with_sin = mixed[(cols + y) * group : (cols + y + 1) * group]
            cu, cv = with_cos[:, :LANES], with_cos[:, LANES:]
            su, sv = with_sin[:, :LANES], with_sin[:, LANES:]
            for slot, value in enumerate((cu - sv, su + cv, cu + sv, su - cv)):
                start = (slot * cols + y) * deep + step * group
                cross[start : start + group, :] = value

    half = cols // 2
    for q in range(2):
        for y0 in range(0, half, 2):
            columns = []
            for dy in range(2):
                pieces = []
                for g in range(2):
                    for r in range(2):
                        start = ((q * 2 + r) * cols + y0 + dy + g * half) * deep
                        pieces.append(cross[start : start + deep, :])
                columns.append(jnp.concatenate(pieces, axis=0).astype(bf16))
            total = jnp.dot(i_mat, jnp.concatenate(columns, axis=1), preferred_element_type=f32)
            for g in range(2):
                re = total[g * 2 * rows : g * 2 * rows + rows]
                im = total[g * 2 * rows + rows : (g + 1) * 2 * rows]
                size = jnp.sqrt(re * re + im * im + eps_mag)
                for dy in range(2):
                    out_ref[
                        y0 + dy + g * half, pl.ds(2 * orient + q, rows, stride=pad), :
                    ] = size[:, dy * LANES : (dy + 1) * LANES]


def filter_features(halo, taps, place, pad):
    _, xlines, rows, cols, samples = halo.shape
    orients = taps.shape[0]
    width = xlines * cols
    sizes = (rows, cols, width, pad, orients)
    return pl.pallas_call(
        functools.partial(filter_kernel, sizes),
        out_shape=jax.ShapeDtypeStruct((cols, rows * pad, samples), f32),
        grid=(orients,),
        in_specs=[
            pl.BlockSpec(memory_space=SMEM),
            pl.BlockSpec(memory_space=SMEM),
            pl.BlockSpec(halo.shape, lambda o: (0,) * 5),
        ],
        out_specs=pl.BlockSpec((cols, rows * pad, samples), lambda o: (0, 0, 0)),
        scratch_shapes=[
            pltpu.VMEM((3 * rows * width, samples), bf16),
            pltpu.VMEM((2 * cols * 8, 8 * width), bf16),
            pltpu.VMEM((4 * cols * 3 * rows, samples), f32),
        ],
        compiler_params=pltpu.CompilerParams(vmem_limit_bytes=50 << 20),
        name="filters",
    )(taps.reshape(-1), place, halo)


def split3(value):
    high = value.astype(bf16)
    rest = value - high.astype(f32)
    mid = rest.astype(bf16)
    low = (rest - mid.astype(f32)).astype(bf16)
    return high, mid, low


def moment_kernel(sizes, with_posterior, feat_ref, shift_ref, mean_ref, var_ref, weight_ref, *rest):
    cols, pad, count, chunk = sizes
    if with_posterior:
        moment_ref, post_ref, table, total, wide = rest
    else:
        moment_ref, table, total = rest
    step = pl.program_id(0)
    comps = mean_ref.shape[0]

    @pl.when(step == 0)
    def _():
        lane = lax.broadcasted_iota(jnp.int32, (comps, 2 * LANES), 1)
        means = jnp.concatenate([mean_ref[...], jnp.zeros((comps, LANES), f32)], axis=1)
        spreads = jnp.concatenate([var_ref[...], jnp.ones((comps, LANES), f32)], axis=1)
        used = lane < count
        inverse = jnp.where(used, 1.0 / spreads, 0.0)
        scaled = means * inverse
        terms = jnp.where(used, jnp.log(2.0 * math.pi * spreads) + means * scaled, 0.0)
        constant = jnp.log(weight_ref[:, :1]) - 0.5 * jnp.sum(terms, axis=1, keepdims=True)
        row = jnp.where(used, scaled, 0.0) + jnp.where(lane == count, constant, 0.0)
        row = row + pltpu.roll(-0.5 * inverse, pad, 1)
        parts = split3(row)
        for index, part in enumerate(parts):
            part = part.astype(f32)
            tiled = part + pltpu.roll(part, 2 * pad, 1) + pltpu.roll(part, 4 * pad, 1)
            table[index * comps : (index + 1) * comps, :] = tiled.astype(bf16)
        total[...] = jnp.zeros_like(total)

    weights = table[:, : 6 * pad]
    for first in range(0, cols, chunk):
        values = jnp.concatenate(
            [feat_ref[first + y] - shift_ref[...] for y in range(chunk)], axis=1
        )
        both = jnp.concatenate([values, values * values], axis=0)
        operand = jnp.concatenate(split3(both), axis=0)
        wide_score = jnp.dot(weights, operand, preferred_element_type=f32)
        score = wide_score[:comps] + (
            wide_score[comps : 2 * comps] + wide_score[2 * comps : 3 * comps]
        )
        exponent = jnp.exp(score - jnp.max(score, axis=0, keepdims=True))
        share = exponent * (1.0 / jnp.sum(exponent, axis=0, keepdims=True))
        high = share.astype(bf16)
        low = (share - high.astype(f32)).astype(bf16)
        total[...] += lax.dot_general(
            jnp.concatenate([high, low], axis=0),
            operand,
            (((1,), (1,)), ((), ())),
            preferred_element_type=f32,
        )
        if with_posterior:
            for y in range(chunk):
                wide[pl.ds(first + y, comps, stride=cols), :] = share[
                    :, y * LANES : (y + 1) * LANES
                ]
    if with_posterior:
        for k in range(comps):
            post_ref[0, k] = wide[k * cols : (k + 1) * cols, :].astype(bf16)

    @pl.when(step == pl.num_programs(0) - 1)
    def _():
        both = total[:comps] + total[comps:]
        both = jnp.concatenate([both, jnp.zeros((comps, 2 * LANES - 6 * pad), f32)], axis=1)
        folded = (
            both
            + pltpu.roll(both, 2 * LANES - 2 * pad, 1)
            + pltpu.roll(both, 2 * LANES - 4 * pad, 1)
        )
        moment_ref[...] = folded[:, :LANES]


def moments(features, shift, params, count, rows, with_posterior):
    means, spreads, weights = params
    comps = means.shape[0]
    cols, flat, samples = features.shape
    pad = flat // rows
    chunk = 4 if cols % 4 == 0 else 1
    whole = lambda array: pl.BlockSpec(array.shape, lambda j: (0, 0))
    out_shape = [jax.ShapeDtypeStruct((comps, LANES), f32)]
    out_specs = [pl.BlockSpec((comps, LANES), lambda j: (0, 0))]
    scratch = [pltpu.VMEM((3 * comps, 2 * LANES), bf16), pltpu.VMEM((2 * comps, 6 * pad), f32)]
    if with_posterior:
        out_shape.append(jax.ShapeDtypeStruct((rows, comps, cols, samples), bf16))
        out_specs.append(pl.BlockSpec((1, comps, cols, samples), lambda j: (j, 0, 0, 0)))
        scratch.append(pltpu.VMEM((comps * cols, samples), f32))
    return pl.pallas_call(
        functools.partial(moment_kernel, (cols, pad, count, chunk), with_posterior),
        out_shape=out_shape,
        grid=(rows,),
        in_specs=[
            pl.BlockSpec((cols, pad, samples), lambda j: (0, j, 0)),
            whole(shift),
            whole(means),
            whole(spreads),
            whole(weights),
        ],
        out_specs=out_specs,
        scratch_shapes=scratch,
        compiler_params=pltpu.CompilerParams(vmem_limit_bytes=50 << 20),
        name="last_pass" if with_posterior else "first_pass",
    )(features, shift, means, spreads, weights)


def update_kernel(
    sizes, moment_ref, mean_ref, var_ref, mean_out, var_out, weight_out, slots, send_sem, recv_sem
):
    inlines, xlines, pad, count, cells = sizes
    members = inlines * xlines
    comps = mean_ref.shape[0]
    me = lax.axis_index("inline") * xlines + lax.axis_index("xline")

    def peer(shift):
        other = lax.rem(me + shift, members)
        return {"inline": other // xlines, "xline": lax.rem(other, xlines)}

    barrier = pltpu.get_barrier_semaphore()
    for shift in range(1, members):
        pl.semaphore_signal(barrier, inc=1, device_id=peer(shift), device_id_type=MESH)
    pl.semaphore_wait(barrier, members - 1)

    def copy(shift):
        return pltpu.make_async_remote_copy(
            src_ref=moment_ref,
            dst_ref=slots.at[me],
            send_sem=send_sem.at[shift],
            recv_sem=recv_sem.at[shift],
            device_id=peer(shift),
            device_id_type=MESH,
        )

    for shift in range(1, members):
        copy(shift).start()
    slots[me] = moment_ref[...]
    for shift in range(1, members):
        copy(shift).wait()
    total = slots[0]
    for member in range(1, members):
        total = total + slots[member]
    mass = total[:, count : count + 1]
    means, spreads = mean_ref[...], var_ref[...]
    used = lax.broadcasted_iota(jnp.int32, (comps, LANES), 1) < count
    first = jnp.where(used, total, 0.0)
    second = jnp.where(used, pltpu.roll(total, LANES - pad, 1), 0.0)
    below = mass + 1.0
    new_means = (first + means) / below
    centred = second - 2.0 * new_means * first + new_means * new_means * mass
    mean_out[...] = new_means
    var_out[...] = jnp.where(used, (centred + spreads) / below, 1.0)
    weight_out[...] = jnp.broadcast_to(below / (cells + comps), (comps, LANES))


def update(moment, params, pad, count, cells, collective_id):
    means, spreads, _ = params
    inlines, xlines = lax.axis_size("inline"), lax.axis_size("xline")
    members = inlines * xlines
    comps = means.shape[0]
    return pl.pallas_call(
        functools.partial(update_kernel, (inlines, xlines, pad, count, cells)),
        out_shape=[jax.ShapeDtypeStruct((comps, LANES), f32)] * 3,
        in_specs=[pl.BlockSpec(memory_space=VMEM)] * 3,
        out_specs=[pl.BlockSpec(memory_space=VMEM)] * 3,
        scratch_shapes=[
            pltpu.VMEM((members, comps, LANES), f32),
            pltpu.SemaphoreType.DMA((members,)),
            pltpu.SemaphoreType.DMA((members,)),
        ],
        compiler_params=pltpu.CompilerParams(
            collective_id=collective_id, has_side_effects=True
        ),
        name="update",
    )(moment, means, spreads)


def per_device(traces, directions, init_means, init_variances, init_weights):
    rows, cols, samples = traces.shape
    assert samples == LANES and rows >= HALF and rows % 8 == 0 and cols % 4 == 0
    orients = directions.shape[0]
    count = 2 * orients
    pad = round_up(count + 1, 8)
    comps = init_weights.shape[0]
    cells = lax.axis_size("inline") * rows * lax.axis_size("xline") * cols * samples
    taps = tap_table(directions)
    place = (lax.axis_index("xline") * cols).astype(jnp.int32).reshape(1)
    shift_row = jnp.mean(init_means, axis=0)
    shift = jnp.broadcast_to(jnp.pad(shift_row, (0, pad - count))[:, None], (pad, LANES))
    halo = gather_halo(traces)
    features = filter_features(halo, taps, place, pad)
    means = jnp.pad(init_means - shift_row, ((0, 0), (0, LANES - count)))
    spreads = jnp.pad(init_variances, ((0, 0), (0, LANES - count)), constant_values=1.0)
    params = (means, spreads, jnp.broadcast_to(init_weights[:, None], (comps, LANES)))
    posterior = None
    for iteration in range(ITERS):
        last = iteration == ITERS - 1
        results = moments(features, shift, params, count, rows, last)
        if last:
            posterior = results[1]
        params = update(results[0], params, pad, count, cells, 1 + iteration)
    means, spreads, weights = params
    return posterior, means[:, :count] + shift_row, spreads[:, :count], weights[:, 0]


def solution(mesh):
    in_specs = (P(("slab", "inline"), "xline", None), P(), P(), P(), P())
    out_specs = (
        P(("slab", "inline"), None, "xline", None),
        P("slab", None),
        P("slab", None),
        P("slab"),
    )
    return jax.shard_map(
        per_device, mesh=mesh, in_specs=in_specs, out_specs=out_specs, check_vma=False
    )
```

```python
import functools
import math

import jax
import jax.numpy as jnp
from jax import lax
from jax.experimental import pallas as pl
from jax.experimental.pallas import tpu as pltpu
from jax.sharding import PartitionSpec as P

TAPS = 31
HALF = 15
AZIMUTHS = 8
DIPS = 4
LANES = 128

eps_mag = 0.01
wavenumber = math.pi / 4.0
width_scale = HALF / 3.0
norm = math.sqrt(
    sum(math.exp(-n * n / (width_scale * width_scale)) for n in range(-HALF, HALF + 1))
)
MESH = pl.DeviceIdType.MESH
f32 = jnp.float32
bf16 = jnp.bfloat16
VMEM = pltpu.MemorySpace.VMEM
SMEM = pltpu.MemorySpace.SMEM


def round_up(value, step):
    return -(-value // step) * step


def halo_kernel(inlines, xlines, own_ref, out_ref, send_sem, recv_sem):
    row = lax.axis_index("inline")
    col = lax.axis_index("xline")

    def there(side):
        return row > 0 if side < 0 else row < inlines - 1

    barrier = pltpu.get_barrier_semaphore()
    for side in (-1, 1):
        @pl.when(there(side))
        def _(side=side):
            pl.semaphore_signal(
                barrier, inc=1, device_id={"inline": row + side}, device_id_type=MESH
            )
    for shift in range(1, xlines):
        pl.semaphore_signal(
            barrier,
            inc=1,
            device_id={"xline": lax.rem(col + shift, xlines)},
            device_id_type=MESH,
        )
    sides = (row > 0).astype(jnp.int32) + (row < inlines - 1).astype(jnp.int32)
    pl.semaphore_wait(barrier, sides + xlines - 1)

    def along(side):
        return pltpu.make_async_remote_copy(
            src_ref=own_ref,
            dst_ref=out_ref.at[1 - side, col],
            send_sem=send_sem.at[1 - side, 0],
            recv_sem=recv_sem.at[1 - side, 0],
            device_id={"inline": row + side},
            device_id_type=MESH,
        )

    def across(block, shift):
        return pltpu.make_async_remote_copy(
            src_ref=own_ref if block == 1 else out_ref.at[block, col],
            dst_ref=out_ref.at[block, col],
            send_sem=send_sem.at[block, shift],
            recv_sem=recv_sem.at[block, shift],
            device_id={"xline": lax.rem(col + shift, xlines)},
            device_id_type=MESH,
        )

    for side in (-1, 1):
        @pl.when(there(side))
        def _(side=side):
            along(side).start()
    for shift in range(1, xlines):
        across(1, shift).start()
    out_ref[1, col] = own_ref[...]
    for side in (-1, 1):
        @pl.when(jnp.logical_not(there(side)))
        def _(side=side):
            out_ref[1 + side] = jnp.zeros(out_ref.shape[1:], out_ref.dtype)
    for side in (-1, 1):
        @pl.when(there(side))
        def _(side=side):
            along(-side).wait_recv()
            for shift in range(1, xlines):
                across(1 + side, shift).start()
    for shift in range(1, xlines):
        across(1, shift).wait()
    for side in (-1, 1):
        @pl.when(there(side))
        def _(side=side):
            along(side).wait_send()
            for shift in range(1, xlines):
                across(1 + side, shift).wait()


def gather_halo(traces):
    inlines, xlines = lax.axis_size("inline"), lax.axis_size("xline")
    return pl.pallas_call(
        functools.partial(halo_kernel, inlines, xlines),
        out_shape=jax.ShapeDtypeStruct((3, xlines) + traces.shape, traces.dtype),
        in_specs=[pl.BlockSpec(memory_space=VMEM)],
        out_specs=pl.BlockSpec(memory_space=VMEM),
        scratch_shapes=[
            pltpu.SemaphoreType.DMA((3, xlines)),
            pltpu.SemaphoreType.DMA((3, xlines)),
        ],
        compiler_params=pltpu.CompilerParams(collective_id=0, has_side_effects=True),
        name="halo",
    )(traces)


def filter_kernel(sizes, dir_ref, halo_ref, out_ref, flat, x_mat, cross):
    rows, cols, width, pad, orients = sizes
    deep = 3 * rows
    group = 8
    orient = pl.program_id(0)

    @pl.when(orient == 0)
    def _():
        for block in range(3):
            for i in range(rows):
                for part in range(width // cols):
                    start = ((block * rows + i) * width) + part * cols
                    flat[start : start + cols, :] = halo_ref[block, part, i]
        for y in range(cols):
            for extra in range(pad - 2 * orients):
                out_ref[y, pl.ds(2 * orients + extra, rows, stride=pad), :] = jnp.full(
                    (rows, LANES), 1.0 if extra == 0 else 0.0, f32
                )

    direction = dir_ref[orient]
    azimuth = jnp.full((8, LANES), (direction % AZIMUTHS).astype(f32)) * (math.pi / AZIMUTHS)
    dip_angle = jnp.full((8, LANES), (direction // AZIMUTHS + 1).astype(f32)) * (
        math.pi / (2 * DIPS + 2)
    )
    waves = [
        wavenumber * (jnp.sin(dip_angle) * jnp.cos(azimuth)),
        wavenumber * (jnp.sin(dip_angle) * jnp.sin(azimuth)),
        wavenumber * jnp.cos(dip_angle),
    ]

    def toeplitz(axis, difference):
        offset = (difference - HALF).astype(f32)
        copies = difference.shape[1] // LANES
        wave = waves[axis]
        phase = offset * (wave if copies == 1 else jnp.concatenate([wave] * copies, axis=1))
        envelope = jnp.exp(-offset * offset / (2.0 * width_scale * width_scale)) / norm
        hit = jnp.logical_and(difference >= 0, difference < TAPS)
        real = jnp.where(hit, envelope * jnp.cos(phase), 0.0)
        imag = jnp.where(hit, envelope * jnp.sin(phase), 0.0)
        return real, imag

    def iotas(shape):
        return (
            lax.broadcasted_iota(jnp.int32, shape, 0),
            lax.broadcasted_iota(jnp.int32, shape, 1),
        )

    def roll(value, amount):
        return value if amount == 0 else pltpu.roll(value, amount, 1)

    sub, lane = iotas((8, LANES))
    bases = toeplitz(2, jnp.bitwise_and(sub - lane + HALF, LANES - 1))
    pieces = []
    for s in range(0, LANES, 8):
        near = jnp.abs(sub + s - lane) <= HALF
        pieces.append(
            jnp.concatenate([jnp.where(near, roll(base, s), 0.0) for base in bases], axis=1)
        )
    time_mat = jnp.concatenate(pieces, axis=0).astype(bf16)

    lanes = round_up(group * width + LANES, LANES)
    sub, lane = iotas((group, lanes))
    difference = lane - sub * width - lax.axis_index("xline") * cols + HALF
    bases = toeplitz(1, jnp.where(difference >= lanes - 64, difference - lanes, difference))
    mine = jnp.logical_and(lane >= sub * width, lane < (sub + 1) * width)
    for part in range(2):
        for y in range(0, cols, 2):
            pair = jnp.concatenate(
                [jnp.where(mine, roll(bases[part], y + dy), 0.0) for dy in range(2)], axis=0
            )
            start = (part * cols + y) * group
            x_mat[start : start + 2 * group, :] = pair[:, : group * width].astype(bf16)

    sub, lane = iotas((8, LANES))
    bases = toeplitz(0, jnp.bitwise_and(lane - sub - rows + HALF, LANES - 1))
    real_first, imag_first = [
        jnp.concatenate(
            [jnp.where(lane < deep, roll(base, j), 0.0) for j in range(0, rows, 8)], axis=0
        )
        for base in bases
    ]
    blank = jnp.zeros((rows, LANES), f32)
    real_first, imag_first = [
        jnp.concatenate([part, blank], axis=1) for part in (real_first, imag_first)
    ]
    real_next, imag_next = pltpu.roll(real_first, deep, 1), pltpu.roll(imag_first, deep, 1)
    base = jnp.concatenate([real_first - imag_next, imag_first + real_next], axis=0)
    i_mat = jnp.concatenate([base, pltpu.roll(base, 2 * deep, 1)], axis=0).astype(bf16)
    i_mat = i_mat[:, : 4 * deep]

    for step in range(deep // group):
        span = group * width
        band = jnp.dot(
            flat[step * span : (step + 1) * span, :],
            time_mat,
            preferred_element_type=f32,
        ).astype(bf16)
        mixed = jnp.dot(x_mat[...], band, preferred_element_type=f32)
        for y in range(cols):
            with_cos = mixed[y * group : (y + 1) * group]
            with_sin = mixed[(cols + y) * group : (cols + y + 1) * group]
            cu, cv = with_cos[:, :LANES], with_cos[:, LANES:]
            su, sv = with_sin[:, :LANES], with_sin[:, LANES:]
            for slot, value in enumerate((cu - sv, su + cv, cu + sv, su - cv)):
                start = (slot * cols + y) * deep + step * group
                cross[start : start + group, :] = value

    half = cols // 2
    for q in range(2):
        for y0 in range(0, half, 2):
            columns = []
            for dy in range(2):
                pieces = []
                for g in range(2):
                    for r in range(2):
                        start = ((q * 2 + r) * cols + y0 + dy + g * half) * deep
                        pieces.append(cross[start : start + deep, :])
                columns.append(jnp.concatenate(pieces, axis=0).astype(bf16))
            total = jnp.dot(i_mat, jnp.concatenate(columns, axis=1), preferred_element_type=f32)
            for g in range(2):
                re = total[g * 2 * rows : g * 2 * rows + rows]
                im = total[g * 2 * rows + rows : (g + 1) * 2 * rows]
                size = jnp.sqrt(re * re + im * im + eps_mag)
                for dy in range(2):
                    out_ref[
                        y0 + dy + g * half, pl.ds(2 * orient + q, rows, stride=pad), :
                    ] = size[:, dy * LANES : (dy + 1) * LANES]


def filter_features(halo, directions, pad):
    _, xlines, rows, cols, samples = halo.shape
    orients = directions.shape[0]
    width = xlines * cols
    sizes = (rows, cols, width, pad, orients)
    return pl.pallas_call(
        functools.partial(filter_kernel, sizes),
        out_shape=jax.ShapeDtypeStruct((cols, rows * pad, samples), f32),
        grid=(orients,),
        in_specs=[
            pl.BlockSpec(memory_space=SMEM),
            pl.BlockSpec(halo.shape, lambda o: (0,) * 5),
        ],
        out_specs=pl.BlockSpec((cols, rows * pad, samples), lambda o: (0, 0, 0)),
        scratch_shapes=[
            pltpu.VMEM((3 * rows * width, samples), bf16),
            pltpu.VMEM((2 * cols * 8, 8 * width), bf16),
            pltpu.VMEM((4 * cols * 3 * rows, samples), f32),
        ],
        compiler_params=pltpu.CompilerParams(vmem_limit_bytes=50 << 20),
        name="filters",
    )(directions, halo)


def split3(value):
    high = value.astype(bf16)
    rest = value - high.astype(f32)
    mid = rest.astype(bf16)
    low = (rest - mid.astype(f32)).astype(bf16)
    return high, mid, low


def column(row):
    return jnp.transpose(jnp.broadcast_to(row, (row.shape[1], row.shape[1])))


def padded(value, fill):
    comps, count = value.shape
    return jnp.concatenate([value, jnp.full((comps, LANES - count), fill, f32)], axis=1)


def first_params(mean_ref, var_ref, weight_ref):
    comps = mean_ref.shape[0]
    means = padded(mean_ref[...], 0.0)
    shift_row = jnp.mean(means, axis=0, keepdims=True)
    weights = column(padded(weight_ref[...], 1.0))[:comps]
    return (means - shift_row, padded(var_ref[...], 1.0), weights), shift_row


def next_params(folded, params, sizes):
    pad, count, cells = sizes
    means, spreads, _ = params
    comps = means.shape[0]
    total = jnp.concatenate([folded, pltpu.roll(folded, LANES // 2, 1)], axis=0)
    used = lax.broadcasted_iota(jnp.int32, (comps, LANES), 1) < count
    mass = total[:, count : count + 1]
    first = jnp.where(used, total, 0.0)
    second = jnp.where(used, pltpu.roll(total, LANES - pad, 1), 0.0)
    below = mass + 1.0
    new_means = (first + means) / below
    centred = second - 2.0 * new_means * first + new_means * new_means * mass
    new_spreads = jnp.where(used, (centred + spreads) / below, 1.0)
    return new_means, new_spreads, jnp.broadcast_to(below / (cells + comps), (comps, LANES))


def peer(shift, inlines, xlines):
    me = lax.axis_index("inline") * xlines + lax.axis_index("xline")
    other = lax.rem(me + shift, inlines * xlines)
    return {"inline": other // xlines, "xline": lax.rem(other, xlines)}


def greet(inlines, xlines):
    barrier = pltpu.get_barrier_semaphore()
    for shift in range(1, inlines * xlines):
        pl.semaphore_signal(
            barrier, inc=1, device_id=peer(shift, inlines, xlines), device_id_type=MESH
        )


def gather_sum(inlines, xlines, payload_ref, slots, send_sem, recv_sem):
    members = inlines * xlines
    me = lax.axis_index("inline") * xlines + lax.axis_index("xline")
    pl.semaphore_wait(pltpu.get_barrier_semaphore(), members - 1)

    def copy(shift):
        return pltpu.make_async_remote_copy(
            src_ref=payload_ref,
            dst_ref=slots.at[me],
            send_sem=send_sem.at[shift],
            recv_sem=recv_sem.at[shift],
            device_id=peer(shift, inlines, xlines),
            device_id_type=MESH,
        )

    for shift in range(1, members):
        copy(shift).start()
    slots[me] = payload_ref[...]
    for shift in range(1, members):
        copy(shift).wait()
    total = slots[0]
    for member in range(1, members):
        total = total + slots[member]
    return total


def gather_scratch(members, comps):
    return [
        pltpu.VMEM((members, comps // 2, LANES), f32),
        pltpu.SemaphoreType.DMA((members,)),
        pltpu.SemaphoreType.DMA((members,)),
    ]


def moment_kernel(sizes, last, *refs):
    cols, pad, count, chunk, together, cells, inlines, xlines = sizes
    if last:
        feat_ref, sum_ref, mean_ref, var_ref, weight_ref, *refs = refs
        moment_ref, post_ref, shift_ref, table, total, wide = refs
    else:
        feat_ref, mean_ref, var_ref, weight_ref, *refs = refs
        moment_ref, shift_ref, table, total, payload, slots, send_sem, recv_sem = refs
    step = pl.program_id(0)
    comps = mean_ref.shape[0]

    @pl.when(step == 0)
    def _():
        if not last:
            greet(inlines, xlines)
        params, shift_row = first_params(mean_ref, var_ref, weight_ref)
        if last:
            params = next_params(sum_ref[...], params, (pad, count, cells))
        shift_ref[...] = column(shift_row)[:pad]
        lane = lax.broadcasted_iota(jnp.int32, (comps, 2 * LANES), 1)
        means = jnp.concatenate([params[0], jnp.zeros((comps, LANES), f32)], axis=1)
        spreads = jnp.concatenate([params[1], jnp.ones((comps, LANES), f32)], axis=1)
        used = lane < count
        inverse = jnp.where(used, 1.0 / spreads, 0.0)
        scaled = means * inverse
        terms = jnp.where(used, jnp.log(2.0 * math.pi * spreads) + means * scaled, 0.0)
        constant = jnp.log(params[2][:, :1]) - 0.5 * jnp.sum(terms, axis=1, keepdims=True)
        row = jnp.where(used, scaled, 0.0) + jnp.where(lane == count, constant, 0.0)
        row = row + pltpu.roll(-0.5 * inverse, pad, 1)
        parts = split3(row)
        for index, part in enumerate(parts):
            part = part.astype(f32)
            tiled = part + pltpu.roll(part, 2 * pad, 1) + pltpu.roll(part, 4 * pad, 1)
            table[index * comps : (index + 1) * comps, :] = tiled.astype(bf16)
        total[...] = jnp.zeros_like(total)

    weights = table[:, : 6 * pad]
    for j in range(together):
        for first in range(0, cols, chunk):
            values = jnp.concatenate(
                [
                    feat_ref[first + y, j * pad : (j + 1) * pad, :] - shift_ref[...]
                    for y in range(chunk)
                ],
                axis=1,
            )
            both = jnp.concatenate([values, values * values], axis=0)
            operand = jnp.concatenate(split3(both), axis=0)
            wide_score = jnp.dot(weights, operand, preferred_element_type=f32)
            score = wide_score[:comps] + (
                wide_score[comps : 2 * comps] + wide_score[2 * comps : 3 * comps]
            )
            exponent = jnp.exp(score - jnp.max(score, axis=0, keepdims=True))
            share = exponent * (1.0 / jnp.sum(exponent, axis=0, keepdims=True))
            high = share.astype(bf16)
            low = (share - high.astype(f32)).astype(bf16)
            total[...] += lax.dot_general(
                jnp.concatenate([high, low], axis=0),
                operand,
                (((1,), (1,)), ((), ())),
                preferred_element_type=f32,
            )
            if last:
                for y in range(chunk):
                    wide[pl.ds((j * comps) * cols + first + y, comps, stride=cols), :] = share[
                        :, y * LANES : (y + 1) * LANES
                    ]
        if last:
            for k in range(comps):
                start = (j * comps + k) * cols
                post_ref[j, k] = wide[start : start + cols, :].astype(bf16)

    @pl.when(step == pl.num_programs(0) - 1)
    def _():
        both = total[:comps] + total[comps:]
        both = jnp.concatenate([both, jnp.zeros((comps, 2 * LANES - 6 * pad), f32)], axis=1)
        summed = (
            both
            + pltpu.roll(both, 2 * LANES - 2 * pad, 1)
            + pltpu.roll(both, 2 * LANES - 4 * pad, 1)
        )[:, :LANES]
        lane = lax.broadcasted_iota(jnp.int32, (comps, LANES), 1)
        summed = jnp.where(lane < 2 * pad, summed, 0.0)
        half = comps // 2
        folded = summed[:half] + pltpu.roll(summed[half:], LANES // 2, 1)
        if last:
            moment_ref[...] = folded
        else:
            payload[...] = folded
            moment_ref[...] = gather_sum(inlines, xlines, payload, slots, send_sem, recv_sem)


def moments(features, summed, init, count, rows, cells):
    last = summed is not None
    inlines, xlines = lax.axis_size("inline"), lax.axis_size("xline")
    comps = init[0].shape[0]
    cols, flat, samples = features.shape
    pad = flat // rows
    assert 4 * pad <= LANES and comps % 16 == 0
    chunk = 4
    together = 2
    folded = jax.ShapeDtypeStruct((comps // 2, LANES), f32)
    inputs = ([summed] if last else []) + list(init)
    out_shape, out_specs = [folded], [pl.BlockSpec(folded.shape, lambda j: (0, 0))]
    scratch = [
        pltpu.VMEM((pad, LANES), f32),
        pltpu.VMEM((3 * comps, 2 * LANES), bf16),
        pltpu.VMEM((2 * comps, 6 * pad), f32),
    ]
    params = dict(vmem_limit_bytes=50 << 20)
    if last:
        out_shape.append(jax.ShapeDtypeStruct((rows, comps, cols, samples), bf16))
        out_specs.append(pl.BlockSpec((together, comps, cols, samples), lambda j: (j, 0, 0, 0)))
        scratch.append(pltpu.VMEM((together * comps * cols, samples), f32))
    else:
        scratch.append(pltpu.VMEM(folded.shape, f32))
        scratch += gather_scratch(inlines * xlines, comps)
        params.update(collective_id=1, has_side_effects=True)
    sizes = (cols, pad, count, chunk, together, cells, inlines, xlines)
    return pl.pallas_call(
        functools.partial(moment_kernel, sizes, last),
        out_shape=out_shape,
        grid=(rows // together,),
        in_specs=[pl.BlockSpec((cols, together * pad, samples), lambda j: (0, j, 0))]
        + [pl.BlockSpec(array.shape, lambda j: (0, 0)) for array in inputs],
        out_specs=out_specs,
        scratch_shapes=scratch,
        compiler_params=pltpu.CompilerParams(**params),
        name="last_pass" if last else "first_pass",
    )(features, *inputs)


def sum_kernel(inlines, xlines, moment_ref, out_ref, slots, send_sem, recv_sem):
    greet(inlines, xlines)
    out_ref[...] = gather_sum(inlines, xlines, moment_ref, slots, send_sem, recv_sem)


def sum_moments(moment):
    inlines, xlines = lax.axis_size("inline"), lax.axis_size("xline")
    return pl.pallas_call(
        functools.partial(sum_kernel, inlines, xlines),
        out_shape=jax.ShapeDtypeStruct(moment.shape, f32),
        in_specs=[pl.BlockSpec(memory_space=VMEM)],
        out_specs=pl.BlockSpec(memory_space=VMEM),
        scratch_shapes=gather_scratch(inlines * xlines, 2 * moment.shape[0]),
        compiler_params=pltpu.CompilerParams(collective_id=2, has_side_effects=True),
        name="sum_moments",
    )(moment)


def final_kernel(sizes, *refs):
    *sums, mean_ref, var_ref, weight_ref, mean_out, var_out, weight_out = refs
    count = sizes[1]
    params, shift_row = first_params(mean_ref, var_ref, weight_ref)
    for summed in sums:
        params = next_params(summed[...], params, sizes)
    means, spreads, weights = params
    comps = means.shape[0]
    mean_out[...] = (means + shift_row)[:, :count]
    var_out[...] = spreads[:, :count]
    square = jnp.concatenate([weights, jnp.zeros((LANES - comps, LANES), f32)], axis=0)
    weight_out[...] = jnp.transpose(square)[:1, :comps]


def finish(sums, init, sizes):
    comps, count = init[0].shape
    inputs = sums + list(init)
    return pl.pallas_call(
        functools.partial(final_kernel, sizes),
        out_shape=[
            jax.ShapeDtypeStruct((comps, count), f32),
            jax.ShapeDtypeStruct((comps, count), f32),
            jax.ShapeDtypeStruct((1, comps), f32),
        ],
        in_specs=[pl.BlockSpec(memory_space=VMEM)] * len(inputs),
        out_specs=[pl.BlockSpec(memory_space=VMEM)] * 3,
        name="finish",
    )(*inputs)


def per_device(traces, directions, init_means, init_variances, init_weights):
    rows, cols, samples = traces.shape
    assert samples == LANES and rows >= HALF and rows % 8 == 0 and cols % 4 == 0
    count = 2 * directions.shape[0]
    pad = round_up(count + 1, 8)
    comps = init_weights.shape[0]
    cells = lax.axis_size("inline") * rows * lax.axis_size("xline") * cols * samples
    init = (init_means, init_variances, init_weights.reshape(1, comps))
    halo = gather_halo(traces)
    features = filter_features(halo, directions, pad)
    (summed,) = moments(features, None, init, count, rows, cells)
    moment, posterior = moments(features, summed, init, count, rows, cells)
    sums = [summed, sum_moments(moment)]
    means, spreads, weights = finish(sums, init, (pad, count, cells))
    return posterior, means, spreads, weights.reshape(comps)


def solution(mesh):
    in_specs = (P(("slab", "inline"), "xline", None), P(), P(), P(), P())
    out_specs = (
        P(("slab", "inline"), None, "xline", None),
        P("slab", None),
        P("slab", None),
        P("slab"),
    )
    return jax.shard_map(
        per_device, mesh=mesh, in_specs=in_specs, out_specs=out_specs, check_vma=False
    )
```

```python
import functools
import math

import jax
import jax.numpy as jnp
from jax import lax
from jax.experimental import pallas as pl
from jax.experimental.pallas import tpu as pltpu
from jax.sharding import PartitionSpec as P

TAPS = 31
HALF = 15
AZIMUTHS = 8
DIPS = 4
LANES = 128

eps_mag = 0.01
wavenumber = math.pi / 4.0
width_scale = HALF / 3.0
norm = math.sqrt(
    sum(math.exp(-n * n / (width_scale * width_scale)) for n in range(-HALF, HALF + 1))
)
MESH = pl.DeviceIdType.MESH
f32 = jnp.float32
bf16 = jnp.bfloat16
VMEM = pltpu.MemorySpace.VMEM
SMEM = pltpu.MemorySpace.SMEM


def round_up(value, step):
    return -(-value // step) * step


def halo_kernel(inlines, xlines, own_ref, out_ref, send_sem, recv_sem):
    row = lax.axis_index("inline")
    col = lax.axis_index("xline")

    def there(side):
        return row > 0 if side < 0 else row < inlines - 1

    barrier = pltpu.get_barrier_semaphore()
    for side in (-1, 1):
        @pl.when(there(side))
        def _(side=side):
            pl.semaphore_signal(
                barrier, inc=1, device_id={"inline": row + side}, device_id_type=MESH
            )
    for shift in range(1, xlines):
        pl.semaphore_signal(
            barrier,
            inc=1,
            device_id={"xline": lax.rem(col + shift, xlines)},
            device_id_type=MESH,
        )
    sides = (row > 0).astype(jnp.int32) + (row < inlines - 1).astype(jnp.int32)
    pl.semaphore_wait(barrier, sides + xlines - 1)

    def along(side):
        return pltpu.make_async_remote_copy(
            src_ref=own_ref,
            dst_ref=out_ref.at[1 - side, col],
            send_sem=send_sem.at[1 - side, 0],
            recv_sem=recv_sem.at[1 - side, 0],
            device_id={"inline": row + side},
            device_id_type=MESH,
        )

    def across(block, shift):
        return pltpu.make_async_remote_copy(
            src_ref=own_ref if block == 1 else out_ref.at[block, col],
            dst_ref=out_ref.at[block, col],
            send_sem=send_sem.at[block, shift],
            recv_sem=recv_sem.at[block, shift],
            device_id={"xline": lax.rem(col + shift, xlines)},
            device_id_type=MESH,
        )

    for side in (-1, 1):
        @pl.when(there(side))
        def _(side=side):
            along(side).start()
    for shift in range(1, xlines):
        across(1, shift).start()
    out_ref[1, col] = own_ref[...]
    for side in (-1, 1):
        @pl.when(jnp.logical_not(there(side)))
        def _(side=side):
            out_ref[1 + side] = jnp.zeros(out_ref.shape[1:], out_ref.dtype)
    for side in (-1, 1):
        @pl.when(there(side))
        def _(side=side):
            along(-side).wait_recv()
            for shift in range(1, xlines):
                across(1 + side, shift).start()
    for shift in range(1, xlines):
        across(1, shift).wait()
    for side in (-1, 1):
        @pl.when(there(side))
        def _(side=side):
            along(side).wait_send()
            for shift in range(1, xlines):
                across(1 + side, shift).wait()


def gather_halo(traces):
    inlines, xlines = lax.axis_size("inline"), lax.axis_size("xline")
    return pl.pallas_call(
        functools.partial(halo_kernel, inlines, xlines),
        out_shape=jax.ShapeDtypeStruct((3, xlines) + traces.shape, traces.dtype),
        in_specs=[pl.BlockSpec(memory_space=VMEM)],
        out_specs=pl.BlockSpec(memory_space=VMEM),
        scratch_shapes=[
            pltpu.SemaphoreType.DMA((3, xlines)),
            pltpu.SemaphoreType.DMA((3, xlines)),
        ],
        compiler_params=pltpu.CompilerParams(
            collective_id=0, has_side_effects=True, vmem_limit_bytes=4 << 20
        ),
        name="halo",
    )(traces)


def filter_kernel(sizes, dir_ref, halo_ref, out_ref, flat, x_mat, cross):
    rows, cols, width, pad, orients = sizes
    deep = 3 * rows
    group = 8
    orient = pl.program_id(0)

    @pl.when(orient == 0)
    def _():
        for block in range(3):
            for i in range(rows):
                for part in range(width // cols):
                    start = ((block * rows + i) * width) + part * cols
                    flat[start : start + cols, :] = halo_ref[block, part, i]
        for y in range(cols):
            for extra in range(pad - 2 * orients):
                out_ref[y, pl.ds(2 * orients + extra, rows, stride=pad), :] = jnp.full(
                    (rows, LANES), 1.0 if extra == 0 else 0.0, f32
                )

    direction = dir_ref[orient]
    azimuth = jnp.full((8, LANES), (direction % AZIMUTHS).astype(f32)) * (math.pi / AZIMUTHS)
    dip_angle = jnp.full((8, LANES), (direction // AZIMUTHS + 1).astype(f32)) * (
        math.pi / (2 * DIPS + 2)
    )
    waves = [
        wavenumber * (jnp.sin(dip_angle) * jnp.cos(azimuth)),
        wavenumber * (jnp.sin(dip_angle) * jnp.sin(azimuth)),
        wavenumber * jnp.cos(dip_angle),
    ]

    def toeplitz(axis, difference):
        offset = (difference - HALF).astype(f32)
        copies = difference.shape[1] // LANES
        wave = waves[axis]
        phase = offset * (wave if copies == 1 else jnp.concatenate([wave] * copies, axis=1))
        envelope = jnp.exp(-offset * offset / (2.0 * width_scale * width_scale)) / norm
        hit = jnp.logical_and(difference >= 0, difference < TAPS)
        real = jnp.where(hit, envelope * jnp.cos(phase), 0.0)
        imag = jnp.where(hit, envelope * jnp.sin(phase), 0.0)
        return real, imag

    def iotas(shape):
        return (
            lax.broadcasted_iota(jnp.int32, shape, 0),
            lax.broadcasted_iota(jnp.int32, shape, 1),
        )

    def roll(value, amount):
        return value if amount == 0 else pltpu.roll(value, amount, 1)

    sub, lane = iotas((8, LANES))
    bases = toeplitz(2, jnp.bitwise_and(sub - lane + HALF, LANES - 1))
    pieces = []
    for s in range(0, LANES, 8):
        near = jnp.abs(sub + s - lane) <= HALF
        pieces.append(
            jnp.concatenate([jnp.where(near, roll(base, s), 0.0) for base in bases], axis=1)
        )
    time_mat = jnp.concatenate(pieces, axis=0).astype(bf16)

    lanes = round_up(group * width + LANES, LANES)
    sub, lane = iotas((group, lanes))
    difference = lane - sub * width - lax.axis_index("xline") * cols + HALF
    bases = toeplitz(1, jnp.where(difference >= lanes - 64, difference - lanes, difference))
    mine = jnp.logical_and(lane >= sub * width, lane < (sub + 1) * width)
    for part in range(2):
        for y in range(0, cols, 2):
            pair = jnp.concatenate(
                [jnp.where(mine, roll(bases[part], y + dy), 0.0) for dy in range(2)], axis=0
            )
            start = (part * cols + y) * group
            x_mat[start : start + 2 * group, :] = pair[:, : group * width].astype(bf16)

    sub, lane = iotas((8, LANES))
    bases = toeplitz(0, jnp.bitwise_and(lane - sub - rows + HALF, LANES - 1))
    real_first, imag_first = [
        jnp.concatenate(
            [jnp.where(lane < deep, roll(base, j), 0.0) for j in range(0, rows, 8)], axis=0
        )
        for base in bases
    ]
    blank = jnp.zeros((rows, LANES), f32)
    real_first, imag_first = [
        jnp.concatenate([part, blank], axis=1) for part in (real_first, imag_first)
    ]
    real_next, imag_next = pltpu.roll(real_first, deep, 1), pltpu.roll(imag_first, deep, 1)
    base = jnp.concatenate([real_first - imag_next, imag_first + real_next], axis=0)
    i_mat = jnp.concatenate([base, pltpu.roll(base, 2 * deep, 1)], axis=0).astype(bf16)
    i_mat = i_mat[:, : 4 * deep]

    for step in range(deep // group):
        span = group * width
        band = jnp.dot(
            flat[step * span : (step + 1) * span, :],
            time_mat,
            preferred_element_type=f32,
        ).astype(bf16)
        mixed = jnp.dot(x_mat[...], band, preferred_element_type=f32)
        for y in range(cols):
            with_cos = mixed[y * group : (y + 1) * group]
            with_sin = mixed[(cols + y) * group : (cols + y + 1) * group]
            cu, cv = with_cos[:, :LANES], with_cos[:, LANES:]
            su, sv = with_sin[:, :LANES], with_sin[:, LANES:]
            for slot, value in enumerate((cu - sv, su + cv, cu + sv, su - cv)):
                start = (slot * cols + y) * deep + step * group
                cross[start : start + group, :] = value

    half = cols // 2
    for q in range(2):
        for y0 in range(0, half, 2):
            columns = []
            for dy in range(2):
                pieces = []
                for g in range(2):
                    for r in range(2):
                        start = ((q * 2 + r) * cols + y0 + dy + g * half) * deep
                        pieces.append(cross[start : start + deep, :])
                columns.append(jnp.concatenate(pieces, axis=0).astype(bf16))
            total = jnp.dot(i_mat, jnp.concatenate(columns, axis=1), preferred_element_type=f32)
            for g in range(2):
                re = total[g * 2 * rows : g * 2 * rows + rows]
                im = total[g * 2 * rows + rows : (g + 1) * 2 * rows]
                size = jnp.sqrt(re * re + im * im + eps_mag)
                for dy in range(2):
                    out_ref[
                        y0 + dy + g * half, pl.ds(2 * orient + q, rows, stride=pad), :
                    ] = size[:, dy * LANES : (dy + 1) * LANES]


def filter_features(halo, directions, pad):
    _, xlines, rows, cols, samples = halo.shape
    orients = directions.shape[0]
    width = xlines * cols
    sizes = (rows, cols, width, pad, orients)
    return pl.pallas_call(
        functools.partial(filter_kernel, sizes),
        out_shape=jax.ShapeDtypeStruct((cols, rows * pad, samples), f32),
        grid=(orients,),
        in_specs=[
            pl.BlockSpec(memory_space=SMEM),
            pl.BlockSpec(memory_space=VMEM),
        ],
        out_specs=pl.BlockSpec(memory_space=VMEM),
        scratch_shapes=[
            pltpu.VMEM((3 * rows * width, samples), bf16),
            pltpu.VMEM((2 * cols * 8, 8 * width), bf16),
            pltpu.VMEM((4 * cols * 3 * rows, samples), f32),
        ],
        compiler_params=pltpu.CompilerParams(vmem_limit_bytes=20 << 20),
        name="filters",
    )(directions, halo)


def split3(value):
    high = value.astype(bf16)
    rest = value - high.astype(f32)
    mid = rest.astype(bf16)
    low = (rest - mid.astype(f32)).astype(bf16)
    return high, mid, low


def column(row):
    return jnp.transpose(jnp.broadcast_to(row, (row.shape[1], row.shape[1])))


def padded(value, fill):
    rows, lanes = value.shape
    wide = jnp.concatenate([value, jnp.full((rows, LANES - lanes), fill, f32)], axis=1)
    full = jnp.concatenate([wide, jnp.full((LANES - rows, LANES), fill, f32)], axis=0)
    return jnp.transpose(full)


def first_params(mean_ref, var_ref, weight_ref):
    comps = mean_ref.shape[1]
    means = padded(mean_ref[...], 0.0)[:comps]
    shift_row = jnp.mean(means, axis=0, keepdims=True)
    weights = jnp.broadcast_to(padded(weight_ref[...], 1.0)[:comps, :1], (comps, LANES))
    return (means - shift_row, padded(var_ref[...], 1.0)[:comps], weights), shift_row


def next_params(folded, params, sizes):
    pad, count, cells = sizes
    means, spreads, _ = params
    comps = means.shape[0]
    total = jnp.concatenate([folded, pltpu.roll(folded, LANES // 2, 1)], axis=0)
    used = lax.broadcasted_iota(jnp.int32, (comps, LANES), 1) < count
    mass = total[:, count : count + 1]
    first = jnp.where(used, total, 0.0)
    second = jnp.where(used, pltpu.roll(total, LANES - pad, 1), 0.0)
    below = mass + 1.0
    new_means = (first + means) / below
    centred = second - 2.0 * new_means * first + new_means * new_means * mass
    new_spreads = jnp.where(used, (centred + spreads) / below, 1.0)
    return new_means, new_spreads, jnp.broadcast_to(below / (cells + comps), (comps, LANES))


def peer(shift, inlines, xlines):
    me = lax.axis_index("inline") * xlines + lax.axis_index("xline")
    other = lax.rem(me + shift, inlines * xlines)
    return {"inline": other // xlines, "xline": lax.rem(other, xlines)}


def greet(inlines, xlines):
    barrier = pltpu.get_barrier_semaphore()
    for shift in range(1, inlines * xlines):
        pl.semaphore_signal(
            barrier, inc=1, device_id=peer(shift, inlines, xlines), device_id_type=MESH
        )


def gather_sum(inlines, xlines, payload_ref, slots, send_sem, recv_sem):
    members = inlines * xlines
    me = lax.axis_index("inline") * xlines + lax.axis_index("xline")
    pl.semaphore_wait(pltpu.get_barrier_semaphore(), members - 1)

    def copy(shift):
        return pltpu.make_async_remote_copy(
            src_ref=payload_ref,
            dst_ref=slots.at[me],
            send_sem=send_sem.at[shift],
            recv_sem=recv_sem.at[shift],
            device_id=peer(shift, inlines, xlines),
            device_id_type=MESH,
        )

    for shift in range(1, members):
        copy(shift).start()
    slots[me] = payload_ref[...]
    for shift in range(1, members):
        copy(shift).wait()
    total = slots[0]
    for member in range(1, members):
        total = total + slots[member]
    return total


def gather_scratch(members, comps):
    return [
        pltpu.VMEM((members, comps // 2, LANES), f32),
        pltpu.SemaphoreType.DMA((members,)),
        pltpu.SemaphoreType.DMA((members,)),
    ]


def moment_kernel(sizes, last, *refs):
    cols, pad, count, chunk, together, cells, inlines, xlines = sizes
    if last:
        split_ref, sum_ref, mean_ref, var_ref, weight_ref, *refs = refs
        moment_ref, post_ref, table, total, wide = refs
    else:
        feat_ref, mean_ref, var_ref, weight_ref, *refs = refs
        moment_ref, split_ref, table, total, shift_ref, payload, slots, send_sem, recv_sem = refs
    step = pl.program_id(0)
    comps = mean_ref.shape[1]

    @pl.when(step == 0)
    def _():
        if not last:
            greet(inlines, xlines)
        params, shift_row = first_params(mean_ref, var_ref, weight_ref)
        if last:
            params = next_params(sum_ref[...], params, (pad, count, cells))
        else:
            shift_ref[...] = column(shift_row)[:pad]
        lane = lax.broadcasted_iota(jnp.int32, (comps, 2 * LANES), 1)
        means = jnp.concatenate([params[0], jnp.zeros((comps, LANES), f32)], axis=1)
        spreads = jnp.concatenate([params[1], jnp.ones((comps, LANES), f32)], axis=1)
        used = lane < count
        inverse = jnp.where(used, 1.0 / spreads, 0.0)
        scaled = means * inverse
        terms = jnp.where(used, jnp.log(2.0 * math.pi * spreads) + means * scaled, 0.0)
        constant = jnp.log(params[2][:, :1]) - 0.5 * jnp.sum(terms, axis=1, keepdims=True)
        row = jnp.where(used, scaled, 0.0) + jnp.where(lane == count, constant, 0.0)
        row = row + pltpu.roll(-0.5 * inverse, pad, 1)
        parts = split3(row)
        for index, part in enumerate(parts):
            part = part.astype(f32)
            tiled = part + pltpu.roll(part, 2 * pad, 1) + pltpu.roll(part, 4 * pad, 1)
            table[index * comps : (index + 1) * comps, :] = tiled.astype(bf16)
        total[...] = jnp.zeros_like(total)

    weights = table[:, : 6 * pad]
    for j in range(together):
        for first in range(0, cols, chunk):
            span = slice(first * LANES, (first + chunk) * LANES)
            if last:
                operand = split_ref[j, :, span]
            else:
                base = pl.multiple_of((step * together + j) * pad, 8)
                values = jnp.concatenate(
                    [
                        feat_ref[first + y, pl.ds(base, pad), :] - shift_ref[...]
                        for y in range(chunk)
                    ],
                    axis=1,
                )
                both = jnp.concatenate([values, values * values], axis=0)
                operand = jnp.concatenate(split3(both), axis=0)
                split_ref[j, :, span] = operand
            wide_score = jnp.dot(weights, operand, preferred_element_type=f32)
            score = wide_score[:comps] + (
                wide_score[comps : 2 * comps] + wide_score[2 * comps : 3 * comps]
            )
            exponent = jnp.exp(score - jnp.max(score, axis=0, keepdims=True))
            share = exponent * (1.0 / jnp.sum(exponent, axis=0, keepdims=True))
            high = share.astype(bf16)
            low = (share - high.astype(f32)).astype(bf16)
            total[...] += lax.dot_general(
                jnp.concatenate([high, low], axis=0),
                operand,
                (((1,), (1,)), ((), ())),
                preferred_element_type=f32,
            )
            if last:
                for y in range(chunk):
                    wide[pl.ds((j * comps) * cols + first + y, comps, stride=cols), :] = share[
                        :, y * LANES : (y + 1) * LANES
                    ]
        if last:
            for k in range(comps):
                start = (j * comps + k) * cols
                post_ref[j, k] = wide[start : start + cols, :].astype(bf16)

    @pl.when(step == pl.num_programs(0) - 1)
    def _():
        both = total[:comps] + total[comps:]
        both = jnp.concatenate([both, jnp.zeros((comps, 2 * LANES - 6 * pad), f32)], axis=1)
        summed = (
            both
            + pltpu.roll(both, 2 * LANES - 2 * pad, 1)
            + pltpu.roll(both, 2 * LANES - 4 * pad, 1)
        )[:, :LANES]
        lane = lax.broadcasted_iota(jnp.int32, (comps, LANES), 1)
        summed = jnp.where(lane < 2 * pad, summed, 0.0)
        half = comps // 2
        folded = summed[:half] + pltpu.roll(summed[half:], LANES // 2, 1)
        if last:
            moment_ref[...] = folded
        else:
            payload[...] = folded
            moment_ref[...] = gather_sum(inlines, xlines, payload, slots, send_sem, recv_sem)


def moments(features, split, summed, init, count, rows, cells):
    last = summed is not None
    inlines, xlines = lax.axis_size("inline"), lax.axis_size("xline")
    comps = init[0].shape[1]
    cols, flat, samples = features.shape
    pad = flat // rows
    assert 4 * pad <= LANES and comps % 16 == 0
    chunk = 4
    together = 2
    folded = jax.ShapeDtypeStruct((comps // 2, LANES), f32)
    inputs = ([summed] if last else []) + list(init)
    out_shape, out_specs = [folded], [pl.BlockSpec(folded.shape, lambda j: (0, 0))]
    split_shape = (rows, 6 * pad, cols * samples)
    split_spec = pl.BlockSpec((together,) + split_shape[1:], lambda j: (j, 0, 0))
    scratch = [
        pltpu.VMEM((3 * comps, 2 * LANES), bf16),
        pltpu.VMEM((2 * comps, 6 * pad), f32),
    ]
    params = dict(vmem_limit_bytes=24 << 20)
    if last:
        out_shape.append(jax.ShapeDtypeStruct((rows, comps, cols, samples), bf16))
        out_specs.append(pl.BlockSpec((together, comps, cols, samples), lambda j: (j, 0, 0, 0)))
        scratch.append(pltpu.VMEM((together * comps * cols, samples), f32))
    else:
        out_shape.append(jax.ShapeDtypeStruct(split_shape, bf16))
        out_specs.append(split_spec)
        scratch += [pltpu.VMEM((pad, LANES), f32), pltpu.VMEM(folded.shape, f32)]
        scratch += gather_scratch(inlines * xlines, comps)
        params.update(collective_id=1, has_side_effects=True)
    sizes = (cols, pad, count, chunk, together, cells, inlines, xlines)
    return pl.pallas_call(
        functools.partial(moment_kernel, sizes, last),
        out_shape=out_shape,
        grid=(rows // together,),
        in_specs=[split_spec if last else pl.BlockSpec(memory_space=VMEM)]
        + [pl.BlockSpec(array.shape, lambda j: (0, 0)) for array in inputs],
        out_specs=out_specs,
        scratch_shapes=scratch,
        compiler_params=pltpu.CompilerParams(**params),
        name="last_pass" if last else "first_pass",
    )(split if last else features, *inputs)


def sum_kernel(inlines, xlines, moment_ref, out_ref, slots, send_sem, recv_sem):
    greet(inlines, xlines)
    out_ref[...] = gather_sum(inlines, xlines, moment_ref, slots, send_sem, recv_sem)


def sum_moments(moment):
    inlines, xlines = lax.axis_size("inline"), lax.axis_size("xline")
    return pl.pallas_call(
        functools.partial(sum_kernel, inlines, xlines),
        out_shape=jax.ShapeDtypeStruct(moment.shape, f32),
        in_specs=[pl.BlockSpec(memory_space=VMEM)],
        out_specs=pl.BlockSpec(memory_space=VMEM),
        scratch_shapes=gather_scratch(inlines * xlines, 2 * moment.shape[0]),
        compiler_params=pltpu.CompilerParams(
            collective_id=2, has_side_effects=True, vmem_limit_bytes=4 << 20
        ),
        name="sum_moments",
    )(moment)


def final_kernel(sizes, *refs):
    *sums, mean_ref, var_ref, weight_ref, mean_out, var_out, weight_out = refs
    count = sizes[1]
    params, shift_row = first_params(mean_ref, var_ref, weight_ref)
    for summed in sums:
        params = next_params(summed[...], params, sizes)
    means, spreads, weights = params
    comps = means.shape[0]
    blank = jnp.zeros((LANES - comps, LANES), f32)
    turned = [
        jnp.transpose(jnp.concatenate([value, blank], axis=0))[:, :comps]
        for value in (means + shift_row, spreads, weights)
    ]
    mean_out[...] = turned[0][:count]
    var_out[...] = turned[1][:count]
    weight_out[...] = turned[2][:1]


def finish(sums, init, sizes):
    count, comps = init[0].shape
    inputs = sums + list(init)
    return pl.pallas_call(
        functools.partial(final_kernel, sizes),
        out_shape=[
            jax.ShapeDtypeStruct((count, comps), f32),
            jax.ShapeDtypeStruct((count, comps), f32),
            jax.ShapeDtypeStruct((1, comps), f32),
        ],
        in_specs=[pl.BlockSpec(memory_space=VMEM)] * len(inputs),
        out_specs=[pl.BlockSpec(memory_space=VMEM)] * 3,
        compiler_params=pltpu.CompilerParams(vmem_limit_bytes=4 << 20),
        name="finish",
    )(*inputs)


def per_device(traces, directions, init_means, init_variances, init_weights):
    rows, cols, samples = traces.shape
    assert samples == LANES and rows >= HALF and rows % 8 == 0 and cols % 4 == 0
    count = 2 * directions.shape[0]
    pad = round_up(count + 1, 8)
    comps = init_weights.shape[0]
    cells = lax.axis_size("inline") * rows * lax.axis_size("xline") * cols * samples
    init = (init_means.T, init_variances.T, init_weights.reshape(1, comps))
    halo = gather_halo(traces)
    features = filter_features(halo, directions, pad)
    summed, split = moments(features, None, None, init, count, rows, cells)
    moment, posterior = moments(features, split, summed, init, count, rows, cells)
    sums = [summed, sum_moments(moment)]
    means, spreads, weights = finish(sums, init, (pad, count, cells))
    return posterior, means.T, spreads.T, weights.reshape(comps)


def solution(mesh):
    in_specs = (P(("slab", "inline"), "xline", None), P(), P(), P(), P())
    out_specs = (
        P(("slab", "inline"), None, "xline", None),
        P("slab", None),
        P("slab", None),
        P("slab"),
    )
    return jax.shard_map(
        per_device, mesh=mesh, in_specs=in_specs, out_specs=out_specs, check_vma=False
    )
```

```python
import functools
import math

import jax
import jax.numpy as jnp
from jax import lax
from jax.experimental import pallas as pl
from jax.experimental.pallas import tpu as pltpu
from jax.sharding import PartitionSpec as P

TAPS = 31
HALF = 15
AZIMUTHS = 8
DIPS = 4
LANES = 128

eps_mag = 0.01
wavenumber = math.pi / 4.0
width_scale = HALF / 3.0
norm = math.sqrt(
    sum(math.exp(-n * n / (width_scale * width_scale)) for n in range(-HALF, HALF + 1))
)
MESH = pl.DeviceIdType.MESH
f32 = jnp.float32
bf16 = jnp.bfloat16
VMEM = pltpu.MemorySpace.VMEM
SMEM = pltpu.MemorySpace.SMEM


def round_up(value, step):
    return -(-value // step) * step


def halo_kernel(inlines, xlines, own_ref, out_ref, send_sem, recv_sem):
    row = lax.axis_index("inline")
    col = lax.axis_index("xline")

    def there(side):
        return row > 0 if side < 0 else row < inlines - 1

    barrier = pltpu.get_barrier_semaphore()
    for side in (-1, 1):
        @pl.when(there(side))
        def _(side=side):
            pl.semaphore_signal(
                barrier, inc=1, device_id={"inline": row + side}, device_id_type=MESH
            )
    for shift in range(1, xlines):
        pl.semaphore_signal(
            barrier,
            inc=1,
            device_id={"xline": lax.rem(col + shift, xlines)},
            device_id_type=MESH,
        )
    sides = (row > 0).astype(jnp.int32) + (row < inlines - 1).astype(jnp.int32)
    pl.semaphore_wait(barrier, sides + xlines - 1)

    def along(side):
        return pltpu.make_async_remote_copy(
            src_ref=own_ref,
            dst_ref=out_ref.at[1 - side, col],
            send_sem=send_sem.at[1 - side, 0],
            recv_sem=recv_sem.at[1 - side, 0],
            device_id={"inline": row + side},
            device_id_type=MESH,
        )

    def across(block, shift):
        return pltpu.make_async_remote_copy(
            src_ref=own_ref if block == 1 else out_ref.at[block, col],
            dst_ref=out_ref.at[block, col],
            send_sem=send_sem.at[block, shift],
            recv_sem=recv_sem.at[block, shift],
            device_id={"xline": lax.rem(col + shift, xlines)},
            device_id_type=MESH,
        )

    for side in (-1, 1):
        @pl.when(there(side))
        def _(side=side):
            along(side).start()
    for shift in range(1, xlines):
        across(1, shift).start()
    out_ref[1, col] = own_ref[...]
    for side in (-1, 1):
        @pl.when(jnp.logical_not(there(side)))
        def _(side=side):
            out_ref[1 + side] = jnp.zeros(out_ref.shape[1:], out_ref.dtype)
    for side in (-1, 1):
        @pl.when(there(side))
        def _(side=side):
            along(-side).wait_recv()
            for shift in range(1, xlines):
                across(1 + side, shift).start()
    for shift in range(1, xlines):
        across(1, shift).wait()
    for side in (-1, 1):
        @pl.when(there(side))
        def _(side=side):
            along(side).wait_send()
            for shift in range(1, xlines):
                across(1 + side, shift).wait()


def gather_halo(traces):
    inlines, xlines = lax.axis_size("inline"), lax.axis_size("xline")
    return pl.pallas_call(
        functools.partial(halo_kernel, inlines, xlines),
        out_shape=jax.ShapeDtypeStruct((3, xlines) + traces.shape, traces.dtype),
        in_specs=[pl.BlockSpec(memory_space=VMEM)],
        out_specs=pl.BlockSpec(memory_space=VMEM),
        scratch_shapes=[
            pltpu.SemaphoreType.DMA((3, xlines)),
            pltpu.SemaphoreType.DMA((3, xlines)),
        ],
        compiler_params=pltpu.CompilerParams(
            collective_id=0, has_side_effects=True, vmem_limit_bytes=4 << 20
        ),
        name="halo",
    )(traces)


def filter_kernel(sizes, dir_ref, halo_ref, out_ref, flat, x_mat, cross):
    rows, cols, width, pad, orients = sizes
    deep = 3 * rows
    group = 8
    orient = pl.program_id(0)

    @pl.when(orient == 0)
    def _():
        for block in range(3):
            for i in range(rows):
                for part in range(width // cols):
                    start = ((block * rows + i) * width) + part * cols
                    flat[start : start + cols, :] = halo_ref[block, part, i]
        for y in range(cols):
            for extra in range(pad - 2 * orients):
                out_ref[y, pl.ds(2 * orients + extra, rows, stride=pad), :] = jnp.full(
                    (rows, LANES), 1.0 if extra == 0 else 0.0, f32
                )

    direction = dir_ref[orient]
    azimuth = jnp.full((8, LANES), (direction % AZIMUTHS).astype(f32)) * (math.pi / AZIMUTHS)
    dip_angle = jnp.full((8, LANES), (direction // AZIMUTHS + 1).astype(f32)) * (
        math.pi / (2 * DIPS + 2)
    )
    waves = [
        wavenumber * (jnp.sin(dip_angle) * jnp.cos(azimuth)),
        wavenumber * (jnp.sin(dip_angle) * jnp.sin(azimuth)),
        wavenumber * jnp.cos(dip_angle),
    ]

    def toeplitz(axis, difference):
        offset = (difference - HALF).astype(f32)
        copies = difference.shape[1] // LANES
        wave = waves[axis]
        phase = offset * (wave if copies == 1 else jnp.concatenate([wave] * copies, axis=1))
        envelope = jnp.exp(-offset * offset / (2.0 * width_scale * width_scale)) / norm
        hit = jnp.logical_and(difference >= 0, difference < TAPS)
        real = jnp.where(hit, envelope * jnp.cos(phase), 0.0)
        imag = jnp.where(hit, envelope * jnp.sin(phase), 0.0)
        return real, imag

    def iotas(shape):
        return (
            lax.broadcasted_iota(jnp.int32, shape, 0),
            lax.broadcasted_iota(jnp.int32, shape, 1),
        )

    def roll(value, amount):
        return value if amount == 0 else pltpu.roll(value, amount, 1)

    sub, lane = iotas((8, LANES))
    bases = toeplitz(2, jnp.bitwise_and(sub - lane + HALF, LANES - 1))
    pieces = []
    for s in range(0, LANES, 8):
        near = jnp.abs(sub + s - lane) <= HALF
        pieces.append(
            jnp.concatenate([jnp.where(near, roll(base, s), 0.0) for base in bases], axis=1)
        )
    time_mat = jnp.concatenate(pieces, axis=0).astype(bf16)

    lanes = round_up(group * width + LANES, LANES)
    sub, lane = iotas((group, lanes))
    difference = lane - sub * width - lax.axis_index("xline") * cols + HALF
    bases = toeplitz(1, jnp.where(difference >= lanes - 64, difference - lanes, difference))
    mine = jnp.logical_and(lane >= sub * width, lane < (sub + 1) * width)
    for part in range(2):
        for y in range(0, cols, 2):
            pair = jnp.concatenate(
                [jnp.where(mine, roll(bases[part], y + dy), 0.0) for dy in range(2)], axis=0
            )
            start = (part * cols + y) * group
            x_mat[start : start + 2 * group, :] = pair[:, : group * width].astype(bf16)

    sub, lane = iotas((8, LANES))
    bases = toeplitz(0, jnp.bitwise_and(lane - sub - rows + HALF, LANES - 1))
    real_first, imag_first = [
        jnp.concatenate(
            [jnp.where(lane < deep, roll(base, j), 0.0) for j in range(0, rows, 8)], axis=0
        )
        for base in bases
    ]
    blank = jnp.zeros((rows, LANES), f32)
    real_first, imag_first = [
        jnp.concatenate([part, blank], axis=1) for part in (real_first, imag_first)
    ]
    real_next, imag_next = pltpu.roll(real_first, deep, 1), pltpu.roll(imag_first, deep, 1)
    base = jnp.concatenate([real_first - imag_next, imag_first + real_next], axis=0)
    i_mat = jnp.concatenate([base, pltpu.roll(base, 2 * deep, 1)], axis=0).astype(bf16)
    i_mat = i_mat[:, : 4 * deep]

    for step in range(deep // group):
        span = group * width
        band = jnp.dot(
            flat[step * span : (step + 1) * span, :],
            time_mat,
            preferred_element_type=f32,
        ).astype(bf16)
        mixed = jnp.dot(x_mat[...], band, preferred_element_type=f32)
        for y in range(cols):
            with_cos = mixed[y * group : (y + 1) * group]
            with_sin = mixed[(cols + y) * group : (cols + y + 1) * group]
            cu, cv = with_cos[:, :LANES], with_cos[:, LANES:]
            su, sv = with_sin[:, :LANES], with_sin[:, LANES:]
            for slot, value in enumerate((cu - sv, su + cv, cu + sv, su - cv)):
                start = (slot * cols + y) * deep + step * group
                cross[start : start + group, :] = value

    half = cols // 2
    for q in range(2):
        for y0 in range(0, half, 2):
            columns = []
            for dy in range(2):
                pieces = []
                for g in range(2):
                    for r in range(2):
                        start = ((q * 2 + r) * cols + y0 + dy + g * half) * deep
                        pieces.append(cross[start : start + deep, :])
                columns.append(jnp.concatenate(pieces, axis=0).astype(bf16))
            total = jnp.dot(i_mat, jnp.concatenate(columns, axis=1), preferred_element_type=f32)
            for g in range(2):
                re = total[g * 2 * rows : g * 2 * rows + rows]
                im = total[g * 2 * rows + rows : (g + 1) * 2 * rows]
                size = jnp.sqrt(re * re + im * im + eps_mag)
                for dy in range(2):
                    out_ref[
                        y0 + dy + g * half, pl.ds(2 * orient + q, rows, stride=pad), :
                    ] = size[:, dy * LANES : (dy + 1) * LANES]


def filter_features(halo, directions, pad):
    _, xlines, rows, cols, samples = halo.shape
    orients = directions.shape[0]
    width = xlines * cols
    sizes = (rows, cols, width, pad, orients)
    return pl.pallas_call(
        functools.partial(filter_kernel, sizes),
        out_shape=jax.ShapeDtypeStruct((cols, rows * pad, samples), f32),
        grid=(orients,),
        in_specs=[
            pl.BlockSpec(memory_space=SMEM),
            pl.BlockSpec(memory_space=VMEM),
        ],
        out_specs=pl.BlockSpec(memory_space=VMEM),
        scratch_shapes=[
            pltpu.VMEM((3 * rows * width, samples), bf16),
            pltpu.VMEM((2 * cols * 8, 8 * width), bf16),
            pltpu.VMEM((4 * cols * 3 * rows, samples), f32),
        ],
        compiler_params=pltpu.CompilerParams(vmem_limit_bytes=20 << 20),
        name="filters",
    )(directions, halo)


def split3(value):
    high = value.astype(bf16)
    rest = value - high.astype(f32)
    mid = rest.astype(bf16)
    low = (rest - mid.astype(f32)).astype(bf16)
    return high, mid, low


def column(row):
    return jnp.transpose(jnp.broadcast_to(row, (row.shape[1], row.shape[1])))


def padded(value, fill):
    rows, lanes = value.shape
    wide = jnp.concatenate([value, jnp.full((rows, LANES - lanes), fill, f32)], axis=1)
    full = jnp.concatenate([wide, jnp.full((LANES - rows, LANES), fill, f32)], axis=0)
    return jnp.transpose(full)


def first_params(mean_ref, var_ref, weight_ref):
    comps = mean_ref.shape[1]
    means = padded(mean_ref[...], 0.0)[:comps]
    shift_row = jnp.mean(means, axis=0, keepdims=True)
    weights = jnp.broadcast_to(padded(weight_ref[...], 1.0)[:comps, :1], (comps, LANES))
    return (means - shift_row, padded(var_ref[...], 1.0)[:comps], weights), shift_row


def next_params(folded, params, sizes):
    pad, count, cells = sizes
    means, spreads, _ = params
    comps = means.shape[0]
    total = jnp.concatenate([folded, pltpu.roll(folded, LANES // 2, 1)], axis=0)
    used = lax.broadcasted_iota(jnp.int32, (comps, LANES), 1) < count
    mass = total[:, count : count + 1]
    first = jnp.where(used, total, 0.0)
    second = jnp.where(used, pltpu.roll(total, LANES - pad, 1), 0.0)
    below = mass + 1.0
    new_means = (first + means) / below
    centred = second - 2.0 * new_means * first + new_means * new_means * mass
    new_spreads = jnp.where(used, (centred + spreads) / below, 1.0)
    return new_means, new_spreads, jnp.broadcast_to(below / (cells + comps), (comps, LANES))


def peer(shift, inlines, xlines):
    me = lax.axis_index("inline") * xlines + lax.axis_index("xline")
    other = lax.rem(me + shift, inlines * xlines)
    return {"inline": other // xlines, "xline": lax.rem(other, xlines)}


def greet(inlines, xlines):
    barrier = pltpu.get_barrier_semaphore()
    for shift in range(1, inlines * xlines):
        pl.semaphore_signal(
            barrier, inc=1, device_id=peer(shift, inlines, xlines), device_id_type=MESH
        )


def gather_sum(inlines, xlines, payload_ref, slots, send_sem, recv_sem):
    members = inlines * xlines
    me = lax.axis_index("inline") * xlines + lax.axis_index("xline")
    pl.semaphore_wait(pltpu.get_barrier_semaphore(), members - 1)

    def copy(shift):
        return pltpu.make_async_remote_copy(
            src_ref=payload_ref,
            dst_ref=slots.at[me],
            send_sem=send_sem.at[shift],
            recv_sem=recv_sem.at[shift],
            device_id=peer(shift, inlines, xlines),
            device_id_type=MESH,
        )

    for shift in range(1, members):
        copy(shift).start()
    slots[me] = payload_ref[...]
    for shift in range(1, members):
        copy(shift).wait()
    total = slots[0]
    for member in range(1, members):
        total = total + slots[member]
    return total


def gather_scratch(members, comps):
    return [
        pltpu.VMEM((members, comps // 2, LANES), f32),
        pltpu.SemaphoreType.DMA((members,)),
        pltpu.SemaphoreType.DMA((members,)),
    ]


def moment_kernel(sizes, last, *refs):
    cols, pad, count, chunk, together, cells, inlines, xlines = sizes
    if last:
        split_ref, sum_ref, mean_ref, var_ref, weight_ref, *refs = refs
        moment_ref, post_ref, table, total, wide = refs
    else:
        feat_ref, mean_ref, var_ref, weight_ref, *refs = refs
        moment_ref, split_ref, table, total, shift_ref, payload, slots, send_sem, recv_sem = refs
    step = pl.program_id(0)
    comps = mean_ref.shape[1]

    @pl.when(step == 0)
    def _():
        if not last:
            greet(inlines, xlines)
        params, shift_row = first_params(mean_ref, var_ref, weight_ref)
        if last:
            params = next_params(sum_ref[...], params, (pad, count, cells))
        else:
            shift_ref[...] = column(shift_row)[:pad]
        lane = lax.broadcasted_iota(jnp.int32, (comps, 2 * LANES), 1)
        means = jnp.concatenate([params[0], jnp.zeros((comps, LANES), f32)], axis=1)
        spreads = jnp.concatenate([params[1], jnp.ones((comps, LANES), f32)], axis=1)
        used = lane < count
        inverse = jnp.where(used, 1.0 / spreads, 0.0)
        scaled = means * inverse
        terms = jnp.where(used, jnp.log(2.0 * math.pi * spreads) + means * scaled, 0.0)
        constant = jnp.log(params[2][:, :1]) - 0.5 * jnp.sum(terms, axis=1, keepdims=True)
        row = jnp.where(used, scaled, 0.0) + jnp.where(lane == count, constant, 0.0)
        row = row + pltpu.roll(-0.5 * inverse, pad, 1)
        parts = split3(row)
        for index, part in enumerate(parts):
            part = part.astype(f32)
            tiled = part + pltpu.roll(part, 2 * pad, 1) + pltpu.roll(part, 4 * pad, 1)
            table[index * comps : (index + 1) * comps, :] = tiled.astype(bf16)
        total[...] = jnp.zeros_like(total)

    weights = table[:, : 6 * pad]
    def scores(j, first):
        span = slice(first * LANES, (first + chunk) * LANES)
        if last:
            operand = split_ref[j, :, span]
        else:
            base = pl.multiple_of((step * together + j) * pad, 8)
            values = jnp.concatenate(
                [
                    feat_ref[first + y, pl.ds(base, pad), :] - shift_ref[...]
                    for y in range(chunk)
                ],
                axis=1,
            )
            both = jnp.concatenate([values, values * values], axis=0)
            operand = jnp.concatenate(split3(both), axis=0)
            split_ref[j, :, span] = operand
        wide_score = jnp.dot(weights, operand, preferred_element_type=f32)
        score = wide_score[:comps] + (
            wide_score[comps : 2 * comps] + wide_score[2 * comps : 3 * comps]
        )
        return operand, score

    pieces = [(j, first) for j in range(together) for first in range(0, cols, chunk)]
    ahead = scores(*pieces[0])
    moment = total[...]
    for index, (j, first) in enumerate(pieces):
        operand, score = ahead
        if index + 1 < len(pieces):
            ahead = scores(*pieces[index + 1])
        exponent = jnp.exp(score - jnp.max(score, axis=0, keepdims=True))
        share = exponent * (1.0 / jnp.sum(exponent, axis=0, keepdims=True))
        high = share.astype(bf16)
        low = (share - high.astype(f32)).astype(bf16)
        moment = moment + lax.dot_general(
            jnp.concatenate([high, low], axis=0),
            operand,
            (((1,), (1,)), ((), ())),
            preferred_element_type=f32,
        )
        if last:
            for y in range(chunk):
                wide[pl.ds((j * comps) * cols + first + y, comps, stride=cols), :] = share[
                    :, y * LANES : (y + 1) * LANES
                ]
    total[...] = moment
    if last:
        for j in range(together):
            for k in range(comps):
                start = (j * comps + k) * cols
                post_ref[j, k] = wide[start : start + cols, :].astype(bf16)

    @pl.when(step == pl.num_programs(0) - 1)
    def _():
        both = total[:comps] + total[comps:]
        both = jnp.concatenate([both, jnp.zeros((comps, 2 * LANES - 6 * pad), f32)], axis=1)
        summed = (
            both
            + pltpu.roll(both, 2 * LANES - 2 * pad, 1)
            + pltpu.roll(both, 2 * LANES - 4 * pad, 1)
        )[:, :LANES]
        lane = lax.broadcasted_iota(jnp.int32, (comps, LANES), 1)
        summed = jnp.where(lane < 2 * pad, summed, 0.0)
        half = comps // 2
        folded = summed[:half] + pltpu.roll(summed[half:], LANES // 2, 1)
        if last:
            moment_ref[...] = folded
        else:
            payload[...] = folded
            moment_ref[...] = gather_sum(inlines, xlines, payload, slots, send_sem, recv_sem)


def moments(features, split, summed, init, count, rows, cells):
    last = summed is not None
    inlines, xlines = lax.axis_size("inline"), lax.axis_size("xline")
    comps = init[0].shape[1]
    cols, flat, samples = features.shape
    pad = flat // rows
    assert 4 * pad <= LANES and comps % 16 == 0
    chunk = 4
    together = 2
    folded = jax.ShapeDtypeStruct((comps // 2, LANES), f32)
    inputs = ([summed] if last else []) + list(init)
    out_shape, out_specs = [folded], [pl.BlockSpec(folded.shape, lambda j: (0, 0))]
    split_shape = (rows, 6 * pad, cols * samples)
    split_spec = pl.BlockSpec((together,) + split_shape[1:], lambda j: (j, 0, 0))
    scratch = [
        pltpu.VMEM((3 * comps, 2 * LANES), bf16),
        pltpu.VMEM((2 * comps, 6 * pad), f32),
    ]
    params = dict(vmem_limit_bytes=24 << 20)
    if last:
        out_shape.append(jax.ShapeDtypeStruct((rows, comps, cols, samples), bf16))
        out_specs.append(pl.BlockSpec((together, comps, cols, samples), lambda j: (j, 0, 0, 0)))
        scratch.append(pltpu.VMEM((together * comps * cols, samples), f32))
    else:
        out_shape.append(jax.ShapeDtypeStruct(split_shape, bf16))
        out_specs.append(split_spec)
        scratch += [pltpu.VMEM((pad, LANES), f32), pltpu.VMEM(folded.shape, f32)]
        scratch += gather_scratch(inlines * xlines, comps)
        params.update(collective_id=1, has_side_effects=True)
    sizes = (cols, pad, count, chunk, together, cells, inlines, xlines)
    return pl.pallas_call(
        functools.partial(moment_kernel, sizes, last),
        out_shape=out_shape,
        grid=(rows // together,),
        in_specs=[split_spec if last else pl.BlockSpec(memory_space=VMEM)]
        + [pl.BlockSpec(array.shape, lambda j: (0, 0)) for array in inputs],
        out_specs=out_specs,
        scratch_shapes=scratch,
        compiler_params=pltpu.CompilerParams(**params),
        name="last_pass" if last else "first_pass",
    )(split if last else features, *inputs)


def sum_kernel(inlines, xlines, moment_ref, out_ref, slots, send_sem, recv_sem):
    greet(inlines, xlines)
    out_ref[...] = gather_sum(inlines, xlines, moment_ref, slots, send_sem, recv_sem)


def sum_moments(moment):
    inlines, xlines = lax.axis_size("inline"), lax.axis_size("xline")
    return pl.pallas_call(
        functools.partial(sum_kernel, inlines, xlines),
        out_shape=jax.ShapeDtypeStruct(moment.shape, f32),
        in_specs=[pl.BlockSpec(memory_space=VMEM)],
        out_specs=pl.BlockSpec(memory_space=VMEM),
        scratch_shapes=gather_scratch(inlines * xlines, 2 * moment.shape[0]),
        compiler_params=pltpu.CompilerParams(
            collective_id=2, has_side_effects=True, vmem_limit_bytes=4 << 20
        ),
        name="sum_moments",
    )(moment)


def final_kernel(sizes, *refs):
    *sums, mean_ref, var_ref, weight_ref, mean_out, var_out, weight_out = refs
    count = sizes[1]
    params, shift_row = first_params(mean_ref, var_ref, weight_ref)
    for summed in sums:
        params = next_params(summed[...], params, sizes)
    means, spreads, weights = params
    comps = means.shape[0]
    blank = jnp.zeros((LANES - comps, LANES), f32)
    turned = [
        jnp.transpose(jnp.concatenate([value, blank], axis=0))[:, :comps]
        for value in (means + shift_row, spreads, weights)
    ]
    mean_out[...] = turned[0][:count]
    var_out[...] = turned[1][:count]
    weight_out[...] = turned[2][:1]


def finish(sums, init, sizes):
    count, comps = init[0].shape
    inputs = sums + list(init)
    return pl.pallas_call(
        functools.partial(final_kernel, sizes),
        out_shape=[
            jax.ShapeDtypeStruct((count, comps), f32),
            jax.ShapeDtypeStruct((count, comps), f32),
            jax.ShapeDtypeStruct((1, comps), f32),
        ],
        in_specs=[pl.BlockSpec(memory_space=VMEM)] * len(inputs),
        out_specs=[pl.BlockSpec(memory_space=VMEM)] * 3,
        compiler_params=pltpu.CompilerParams(vmem_limit_bytes=4 << 20),
        name="finish",
    )(*inputs)


def per_device(traces, directions, init_means, init_variances, init_weights):
    rows, cols, samples = traces.shape
    assert samples == LANES and rows >= HALF and rows % 8 == 0 and cols % 4 == 0
    count = 2 * directions.shape[0]
    pad = round_up(count + 1, 8)
    comps = init_weights.shape[0]
    cells = lax.axis_size("inline") * rows * lax.axis_size("xline") * cols * samples
    init = (init_means.T, init_variances.T, init_weights.reshape(1, comps))
    halo = gather_halo(traces)
    features = filter_features(halo, directions, pad)
    summed, split = moments(features, None, None, init, count, rows, cells)
    moment, posterior = moments(features, split, summed, init, count, rows, cells)
    sums = [summed, sum_moments(moment)]
    means, spreads, weights = finish(sums, init, (pad, count, cells))
    return posterior, means.T, spreads.T, weights.reshape(comps)


def solution(mesh):
    in_specs = (P(("slab", "inline"), "xline", None), P(), P(), P(), P())
    out_specs = (
        P(("slab", "inline"), None, "xline", None),
        P("slab", None),
        P("slab", None),
        P("slab"),
    )
    return jax.shard_map(
        per_device, mesh=mesh, in_specs=in_specs, out_specs=out_specs, check_vma=False
    )
```
